128 devices in a mesh: req: 4 (over y), seq: 32 (over x, z, core).
Axes of the slice: x: 4, y: 4, z: 4, core: 2. Of those that a mesh axis runs over, the one named last changes fastest.
Arguments:
- tokens: bfloat16 [4, 4096, 2048], P('req', 'seq'), may hold values from -6 to 6
- lengths: int32 [4, 4], replicated, may hold values from 1 to 2048, as said below
- attn_gain: bfloat16 [2048], replicated, may hold values from 0.099609375 to 1.8984375
- w_query: bfloat16 [2048, 512], replicated, may hold values from -0.125 to 0.125
- w_key: bfloat16 [2048, 512], replicated, may hold values from -0.125 to 0.125
- w_value: bfloat16 [2048, 1024], replicated, may hold values from -0.125 to 0.125
- w_outgate: bfloat16 [2048, 1024], replicated, may hold values from -0.125 to 0.125
- gate_down: bfloat16 [2048, 16], replicated, may hold values from -1 to 1
- gate_up: bfloat16 [16, 512], replicated, may hold values from -2 to 2
- gate_bias: float32 [512], replicated, may hold values from -1 to 8
- conv_weight: bfloat16 [4, 2048], replicated, may hold values from -2 to 2
- head_gain: bfloat16 [512], replicated, may hold values from 0.099609375 to 1.8984375
- w_out: bfloat16 [1024, 2048], replicated, may hold values from -0.1875 to 0.1875
- forward_norm_scale: bfloat16 [2048], replicated, may hold values from 0.099609375 to 1.8984375
- w_gate: bfloat16 [2048, 2816], P('seq', 'req'), may hold values from -0.125 to 0.125
- w_up: bfloat16 [2048, 2816], P('seq', 'req'), may hold values from -0.125 to 0.125
- down_weight: bfloat16 [2048, 2816], P('seq', 'req'), may hold values from -0.109375 to 0.109375
Outputs:
- output: bfloat16 [4, 4096, 2048], P('req', 'seq')
The draws below stay inside these ranges and needn't reach their ends.
Inputs may be any that keep to these rules, and one draw needn't show every extreme that they name: Row g lists the prompt lengths of group g's 4 requests, packed in slot order from position 0 of the group; every row holds one length equal to 2048; rows 2i and 2i + 1 together sum to 6144, so all rows sum to 12288; each row sums to between 2052 and 4092.
All inputs are finite; a program needn't handle non-finite values.
Results may differ from the reference program's by a relative error of at most 0.008.
Values may be sent and summed in bfloat16 or wider, within the bound.
A program may use at most 128 MiB of HBM per device.

```python
import jax
import jax.numpy as jnp
from jax import lax

D = 2048
DVH = 512
RANK = 16
HEADS = 2
FF = 2816
TAPS = 4
SPAN = 64
REQS = 4
DK = 512
DV = 1024
GROUPS = 4
STREAM = 4096
MAXLEN = 2048


def draw_lengths(key, part):
    key_shift, key_weight, key_order = jax.random.split(key, 3)
    pair_count = GROUPS // 2
    shift_amount = jax.random.randint(key_shift, (pair_count,), 0, STREAM // 4 - REQS + 1)
    middle = 3 * STREAM // 4
    totals = jnp.stack([middle + shift_amount, middle - shift_amount], axis=1).reshape(GROUPS)
    remainder = totals - MAXLEN - (REQS - 1)
    weights = jax.random.randint(key_weight, (GROUPS, REQS - 1), 1, 1000)
    shares = remainder[:, None] * weights // jnp.sum(weights, axis=1, keepdims=True)
    leading = shares[:, :-1]
    closing = remainder - jnp.sum(leading, axis=1)
    parts_all = jnp.concatenate([leading, closing[:, None]], axis=1) + 1
    filled = jnp.concatenate([parts_all, jnp.full((GROUPS, 1), MAXLEN, jnp.int32)], axis=1)
    order_keys = jax.random.split(key_order, GROUPS)
    orders = jax.vmap(lambda row_key: jax.random.permutation(row_key, REQS))(order_keys)
    return jnp.take_along_axis(filled, orders, axis=1).astype(jnp.int32)


def draw_gate_down(key, part):
    noise = jnp.clip(jax.random.normal(jax.random.fold_in(key, 101), (D, RANK), jnp.float32), -6.0, 6.0) * D ** (-0.5)
    return jnp.clip(noise, -1.0, 1.0).astype(jnp.bfloat16)


def draw_gate_up(key, part):
    noise = jnp.clip(jax.random.normal(jax.random.fold_in(key, 102), (RANK, DK), jnp.float32), -4.0, 4.0)
    value = 0.5 * noise
    return jnp.clip(value, -2.0, 2.0).astype(jnp.bfloat16)


def draw_tokens(key, part):
    starting_index = jnp.clip(jax.random.normal(jax.random.fold_in(key, 106), (GROUPS, STREAM, D), jnp.float32), -6.0, 6.0)
    return starting_index.astype(jnp.bfloat16)


def draw_gate_bias(key, part):
    folded = jax.random.fold_in(key, 107)
    key_pick, key_fast, key_slow = jax.random.split(folded, 3)
    picks = jax.random.uniform(key_pick, (DK,)) < 0.5
    fast = jax.random.uniform(key_fast, (DK,), minval=-1.0, maxval=2.0)
    slow = jax.random.uniform(key_slow, (DK,), minval=5.0, maxval=8.0)
    return jnp.where(picks, slow, fast).astype(jnp.float32)


def block_levels(own_key, dims, pieces, least, high):
    factor_of = 1.0
    for dim, parts in pieces:
        heights = jax.random.uniform(jax.random.fold_in(jax.random.fold_in(own_key, 6), dim), (parts,), jnp.float32, least / len(pieces), high / len(pieces))
        factor_of = factor_of * jnp.repeat(jnp.exp(heights), dims[dim] // parts).reshape((-1,) + (1,) * (len(dims) - 1 - dim))
    return factor_of


def scatter_about(rng, extent, deviation, reach, cuts=(), kind=jnp.bfloat16):
    result = deviation * jax.random.normal(rng, extent, jnp.float32)
    if cuts:
        result = result * block_levels(rng, extent, cuts, -0.22, 0.18)
    return jnp.clip(result, -reach, reach).astype(kind)


def setup_inputs(seed: int = 0) -> dict:
    key_list = jax.random.split(jax.random.key(seed), 18)
    return {
        "tokens": draw_tokens(jax.random.fold_in(key_list[17], 71), 0),
        "lengths": draw_lengths(jax.random.fold_in(key_list[17], 71), 0),
        "attn_gain": jnp.clip(1.0 + 0.18 * jax.random.normal(key_list[2], (D,), jnp.float32), 0.099609375, 1.8984375).astype(jnp.bfloat16),
        "w_query": scatter_about(key_list[3], (D, DK), D ** -0.5, 0.125),
        "w_key": scatter_about(key_list[4], (D, DK), D ** -0.5, 0.125),
        "w_value": scatter_about(key_list[5], (D, DV), D ** -0.5, 0.125),
        "w_outgate": scatter_about(key_list[6], (D, DV), D ** -0.5, 0.125),
        "gate_down": draw_gate_down(jax.random.fold_in(key_list[17], 71), 0),
        "gate_up": draw_gate_up(jax.random.fold_in(key_list[17], 71), 0),
        "gate_bias": draw_gate_bias(jax.random.fold_in(key_list[17], 71), 0),
        "conv_weight": scatter_about(key_list[10], (TAPS, 2 * DK + DV), 0.5, 2.0),
        "head_gain": jnp.clip(1.0 + 0.18 * jax.random.normal(key_list[11], (DVH,), jnp.float32), 0.099609375, 1.8984375).astype(jnp.bfloat16),
        "w_out": scatter_about(key_list[12], (DV, D), DV ** -0.5, 0.1875),
        "forward_norm_scale": jnp.clip(1.0 + 0.18 * jax.random.normal(key_list[13], (D,), jnp.float32), 0.099609375, 1.8984375).astype(jnp.bfloat16),
        "w_gate": scatter_about(key_list[14], (D, FF), D ** -0.5, 0.125, ((0, 32), (1, 4))),
        "w_up": scatter_about(key_list[15], (D, FF), D ** -0.5, 0.125, ((0, 32), (1, 4))),
        "down_weight": scatter_about(key_list[16], (D, FF), FF ** -0.5, 0.109375, ((0, 32), (1, 4))),
    }


EPSILON = 1e-05
NORMALIZER = 16.0
MAXIMUM_ACCURACY = lax.Precision.HIGHEST

def rms_scale(values, gain):
    mean_square = lax.optimization_barrier(jnp.mean(values * values, axis=-1, keepdims=True))
    return values * lax.rsqrt(mean_square + EPSILON) * gain

def segment_ids(positions, bounds):
    return lax.optimization_barrier(jnp.sum((positions[:, None] >= bounds[None, :]).astype(jnp.int32), axis=1))

def short_conv(extended, segment_ext, conv_weight, count):
    taps = conv_weight.shape[0]
    own_segment = segment_ext[taps - 1:]
    total = jnp.zeros((count, extended.shape[1]), jnp.float32)
    for tap_index in range(taps):
        first = taps - 1 - tap_index
        shifted = extended[first:first + count].astype(jnp.float32)
        same = (segment_ext[first:first + count] == own_segment).astype(jnp.float32)
        total = total + conv_weight[tap_index].astype(jnp.float32) * shifted * same[:, None]
    return total

def span_cumulative(log_decay):
    span_len, head_count, key_width = log_decay.shape
    lower = jnp.tril(jnp.ones((span_len, span_len), jnp.float32))
    flat = jnp.dot(lower, log_decay.reshape(span_len, head_count * key_width), precision=MAXIMUM_ACCURACY)
    return flat.reshape(span_len, head_count, key_width)

def state_update(recurrent_state, cumulative, keys_float, value_rows_wide, segment_span, clean_last):
    tail = cumulative[-1]
    keep = (segment_span == segment_span[-1]).astype(jnp.float32)
    weighted_values = keys_float * jnp.exp(tail[None] - cumulative) * keep[:, None, None]
    state_increment = jnp.einsum('ugl,ugi->gli', weighted_values, value_rows_wide, precision=MAXIMUM_ACCURACY)
    return recurrent_state * (jnp.exp(tail) * clean_last)[:, :, None] + state_increment

def span_attend(recurrent_state, items):
    query, keys, values, log_decay, segment_span, segment_before = items
    cumulative = span_cumulative(log_decay)
    query_float = query.astype(jnp.float32)
    keys_float = keys.astype(jnp.float32)
    value_rows_wide = values.astype(jnp.float32)
    clean = (segment_span == segment_before).astype(jnp.float32)
    query_decayed_rows = query_float * jnp.exp(cumulative) * clean[:, None, None]
    carried_forward = jnp.einsum('ynj,njc->ync', query_decayed_rows, recurrent_state, precision=MAXIMUM_ACCURACY)
    order = jnp.arange(segment_span.shape[0])
    allowed = (segment_span[:, None] == segment_span[None, :]) & (order[:, None] >= order[None, :])
    gap = jnp.where(allowed[:, :, None, None], cumulative[:, None] - cumulative[None, :], 0.0)
    scores = lax.optimization_barrier(jnp.sum(query_float[:, None] * keys_float[None, :] * jnp.exp(gap), axis=-1))
    scores = scores * allowed[:, :, None].astype(jnp.float32)
    scores_low = scores.astype(jnp.bfloat16)
    inner = jnp.einsum('tsh,shv->thv', scores_low.astype(jnp.float32), value_rows_wide)
    new_state = state_update(recurrent_state, cumulative, keys_float, value_rows_wide, segment_span, clean[-1])
    return (new_state, carried_forward + inner)

def reference(tokens, lengths, attn_gain, w_query, w_key, w_value, w_outgate, gate_down, gate_up, gate_bias, conv_weight, head_gain, w_out, forward_norm_scale, w_gate, w_up, down_weight):
    bounds_all = jnp.cumsum(lengths, axis=1).astype(jnp.int32)
    key_total = w_query.shape[1]
    value_total = w_value.shape[1]
    key_width = key_total // HEADS
    value_width = value_total // HEADS
    span_count = STREAM // SPAN
    results = []
    for group_index in range(GROUPS):
        inputs = tokens[group_index]
        bounds = bounds_all[group_index]
        positions = jnp.arange(STREAM, dtype=jnp.int32)
        segment = segment_ids(positions, bounds)
        valid = segment < lengths.shape[1]
        normed = rms_scale(inputs.astype(jnp.float32), attn_gain.astype(jnp.float32)).astype(jnp.bfloat16)
        projected = jnp.concatenate([jnp.dot(normed, w_query, preferred_element_type=jnp.float32), jnp.dot(normed, w_key, preferred_element_type=jnp.float32), jnp.dot(normed, w_value, preferred_element_type=jnp.float32)], axis=1).astype(jnp.bfloat16)
        outgate = jnp.dot(normed, w_outgate, preferred_element_type=jnp.float32)
        latent = jnp.dot(normed, gate_down, preferred_element_type=jnp.float32)
        logits = jnp.dot(latent, gate_up.astype(jnp.float32), precision=MAXIMUM_ACCURACY) + gate_bias
        log_decay = jax.nn.log_sigmoid(logits) / NORMALIZER
        extended = jnp.concatenate([jnp.zeros((TAPS - 1, projected.shape[1]), jnp.bfloat16), projected], axis=0)
        segment_ext = jnp.concatenate([jnp.full((TAPS - 1,), -1, jnp.int32), segment], axis=0)
        convolved = jax.nn.silu(short_conv(extended, segment_ext, conv_weight, STREAM)).astype(jnp.bfloat16)
        query = convolved[:, :key_total].reshape(span_count, SPAN, HEADS, key_width)
        keys = convolved[:, key_total:2 * key_total].reshape(span_count, SPAN, HEADS, key_width)
        values = convolved[:, 2 * key_total:].reshape(span_count, SPAN, HEADS, value_width)
        decay_spans = log_decay.reshape(span_count, SPAN, HEADS, key_width)
        segment_spans = segment.reshape(span_count, SPAN)
        segment_before = jnp.concatenate([jnp.full((1,), -1, jnp.int32), segment_spans[:-1, -1]], axis=0)
        zero_state = jnp.zeros((HEADS, key_width, value_width), jnp.float32)
        final_state, attended = lax.scan(span_attend, zero_state, (query, keys, values, decay_spans, segment_spans, segment_before))
        attended = attended.reshape(STREAM, HEADS, value_width)
        gated = rms_scale(attended, head_gain.astype(jnp.float32)).reshape(STREAM, value_total) * jax.nn.silu(outgate)
        resident = (jnp.dot(gated.astype(jnp.bfloat16), w_out, preferred_element_type=jnp.float32) + inputs.astype(jnp.float32)).astype(jnp.bfloat16)
        mlp_normed = rms_scale(resident.astype(jnp.float32), forward_norm_scale.astype(jnp.float32)).astype(jnp.bfloat16)
        gate = jnp.dot(mlp_normed, w_gate, preferred_element_type=jnp.float32)
        upward = jnp.dot(mlp_normed, w_up, preferred_element_type=jnp.float32)
        hidden = (jax.nn.silu(gate) * upward).astype(jnp.bfloat16)
        mlp_out = jnp.dot(hidden, down_weight.T, preferred_element_type=jnp.float32).astype(jnp.bfloat16)
        output = jnp.where(valid[:, None], resident.astype(jnp.float32) + mlp_out.astype(jnp.float32), 0.0).astype(jnp.bfloat16)
        results.append(output)
    return jnp.stack(results, axis=0)
```

```python
import functools

import jax
import jax.numpy as jnp
from jax import lax
from jax.experimental import pallas as pl
from jax.experimental.pallas import tpu as pltpu
from jax.sharding import PartitionSpec as P

HEADS = 2
EPSILON = 1e-05
NORMALIZER = 16.0
HIGHEST = lax.Precision.HIGHEST
MESH = pl.DeviceIdType.MESH

SIDE = 4
BLOCKS = SIDE**3
HALF = 384
ORDERS = (("x", "y", "z"), ("y", "z", "x"), ("z", "x", "y"))


def place():
    seq = lax.axis_index("seq")
    return {
        "x": seq // (2 * SIDE),
        "z": (seq // 2) % SIDE,
        "y": lax.axis_index("req"),
        "c": seq % 2,
    }


def device_at(at):
    return (at["y"], (at["x"] * SIDE + at["z"]) * 2 + at["c"])


def moved(at, axis, by):
    new = dict(at)
    new[axis] = (at[axis] + by + SIDE) % SIDE
    return new


def block_of(at):
    return at["y"] * (SIDE * SIDE) + at["x"] * SIDE + at["z"]


def gather_kernel(rows, *refs):
    shards, fulls = refs[:3], refs[3:6]
    local_sem, pair_send, pair_recv, send_sem, recv_sem = refs[6:]
    me = place()
    core = me["c"]
    sibling = dict(me, c=1 - core)
    barrier = pltpu.get_barrier_semaphore()
    partners = [moved(me, axis, by) for axis in "xyz" for by in (1, -1)] + [sibling]
    for partner in partners:
        pl.semaphore_signal(barrier, inc=1, device_id=device_at(partner), device_id_type=MESH)
    pl.semaphore_wait(barrier, len(partners))

    def slot(part, at):
        return fulls[part].at[pl.ds(pl.multiple_of(block_of(at) * 2 * rows, 128), 2 * rows), :]

    def half(part, at, source_core):
        first = pl.multiple_of((block_of(at) * 2 + source_core) * rows, 64)
        return fulls[part].at[pl.ds(first, rows), :]

    def columns(part, which):
        return shards[part].at[:, pl.ds(pl.multiple_of(which * HALF, 128), HALF)]

    locals_, pairs = [], []
    for part in range(3):
        pair = pltpu.make_async_remote_copy(
            src_ref=columns(part, 1 - core),
            dst_ref=half(part, me, core),
            send_sem=pair_send.at[part],
            recv_sem=pair_recv.at[part],
            device_id=device_at(sibling),
            device_id_type=MESH,
        )
        pair.start()
        pairs.append(pair)
        own = pltpu.make_async_copy(columns(part, core), half(part, me, core), local_sem.at[part])
        own.start()
        locals_.append(own)

    def send(part, at, axis, by):
        pltpu.make_async_remote_copy(
            src_ref=slot(part, at),
            dst_ref=slot(part, at),
            send_sem=send_sem.at[part],
            recv_sem=recv_sem.at[part, block_of(at)],
            device_id=device_at(moved(me, axis, by)),
            device_id_type=MESH,
        ).start()

    def arrive(part, at):
        pltpu.make_async_remote_copy(
            src_ref=slot(part, at),
            dst_ref=slot(part, at),
            send_sem=send_sem.at[part],
            recv_sem=recv_sem.at[part, block_of(at)],
            device_id=device_at(sibling),
            device_id_type=MESH,
        ).wait_recv()

    def both(part, at, axis):
        send(part, at, axis, 1)
        send(part, at, axis, -1)

    onward = 1 - 2 * core

    for part in range(3):
        locals_[part].wait()
        pairs[part].wait_recv()
        both(part, me, ORDERS[part][0])
    for part in range(3):
        both(part, me, ORDERS[part][1])
    for part in range(3):
        both(part, me, ORDERS[part][2])

    for kind, by in enumerate((-onward, onward, 2)):
        for part in range(3):
            first, second, third = ORDERS[part]
            at = dict(me)
            at[first] = (me[first] + by + SIDE) % SIDE
            arrive(part, at)
            if kind == 0:
                send(part, at, first, onward)
            both(part, at, second)
            both(part, at, third)

    for kind, by in enumerate((-onward, onward, 2)):
        def along_first(step, carry, kind=kind, by=by):
            for part in range(3):
                first, second, third = ORDERS[part]
                at = dict(me)
                at[first] = (me[first] + step) % SIDE
                at[second] = (me[second] + by + SIDE) % SIDE
                arrive(part, at)
                if kind == 0:
                    send(part, at, second, onward)
                both(part, at, third)
            return carry

        lax.fori_loop(0, SIDE, along_first, 0)

    for kind, by in enumerate((-onward, onward, 2)):
        def along_two(step, carry, kind=kind, by=by):
            for part in range(3):
                first, second, third = ORDERS[part]
                at = dict(me)
                at[first] = (me[first] + step % SIDE) % SIDE
                at[second] = (me[second] + step // SIDE) % SIDE
                at[third] = (me[third] + by + SIDE) % SIDE
                arrive(part, at)
                if kind == 0:
                    send(part, at, third, onward)
            return carry

        lax.fori_loop(0, SIDE * SIDE, along_two, 0)

    for part in range(3):
        pairs[part].wait_send()
        sent = fulls[part].at[pl.ds(0, (BLOCKS - 1) * 2 * rows), :]
        pltpu.make_async_remote_copy(
            src_ref=sent,
            dst_ref=sent,
            send_sem=send_sem.at[part],
            recv_sem=recv_sem.at[part, 0],
            device_id=device_at(sibling),
            device_id_type=MESH,
        ).wait_send()


def gather_weights(shards):
    rows = shards[0].shape[0]
    padded = [jnp.pad(shard, ((0, 0), (0, 2 * HALF - shard.shape[1]))) for shard in shards]
    any_spec = pl.BlockSpec(memory_space=pl.ANY)
    full = jax.ShapeDtypeStruct((BLOCKS * 2 * rows, HALF), jnp.bfloat16)
    return pl.pallas_call(
        functools.partial(gather_kernel, rows),
        out_shape=[full] * 3,
        in_specs=[any_spec] * 3,
        out_specs=[any_spec] * 3,
        scratch_shapes=[
            pltpu.SemaphoreType.DMA((3,)),
            pltpu.SemaphoreType.DMA((3,)),
            pltpu.SemaphoreType.DMA((3,)),
            pltpu.SemaphoreType.DMA((3,)),
            pltpu.SemaphoreType.DMA((3, BLOCKS)),
        ],
        compiler_params=pltpu.CompilerParams(collective_id=0, has_side_effects=True),
        name="gather_weights",
    )(*padded)


def from_behind(value, axis, steps):
    count = lax.axis_size(axis)
    return lax.ppermute(value, axis, [(source, source + steps) for source in range(count - steps)])


def rms_scale(values, gain):
    mean_square = jnp.mean(values * values, axis=-1, keepdims=True)
    return values * lax.rsqrt(mean_square + EPSILON) * gain


def segment_ids(positions, bounds):
    return jnp.sum((positions[:, None] >= bounds[None, :]).astype(jnp.int32), axis=1)


def short_conv(extended, segment_ext, conv_weight, count):
    taps = conv_weight.shape[0]
    own_segment = segment_ext[taps - 1 :]
    total = jnp.zeros((count, extended.shape[1]), jnp.float32)
    for tap_index in range(taps):
        first = taps - 1 - tap_index
        shifted = extended[first : first + count].astype(jnp.float32)
        same = (segment_ext[first : first + count] == own_segment).astype(jnp.float32)
        total = total + conv_weight[tap_index].astype(jnp.float32) * shifted * same[:, None]
    return total


def shards(
    tokens,
    lengths,
    attn_gain,
    w_query,
    w_key,
    w_value,
    w_outgate,
    gate_down,
    gate_up,
    gate_bias,
    conv_weight,
    head_gain,
    w_out,
    forward_norm_scale,
    w_gate,
    w_up,
    down_weight,
):
    gate_all, up_all, down_all = gather_weights((w_gate, w_up, down_weight))
    devices = lax.axis_size("seq")
    group_index = lax.axis_index("req")
    slice_index = lax.axis_index("seq")
    inputs = tokens[0]
    block_rows = inputs.shape[0]
    request_slots = lengths.shape[1]
    bounds_all = jnp.cumsum(lengths, axis=1)
    group_row = jnp.arange(lengths.shape[0], dtype=jnp.int32) == group_index
    bounds = jnp.sum(jnp.where(group_row[:, None], bounds_all, 0), axis=0)
    start_pos = slice_index * block_rows
    taps = conv_weight.shape[0]
    segment_ext = segment_ids(
        start_pos - (taps - 1) + jnp.arange(block_rows + taps - 1, dtype=jnp.int32), bounds
    )
    segment = segment_ext[taps - 1 :]
    segment_before = segment_ext[taps - 2]
    valid = segment < request_slots
    normed = rms_scale(inputs.astype(jnp.float32), attn_gain.astype(jnp.float32)).astype(
        jnp.bfloat16
    )
    projected = jnp.concatenate(
        [
            jnp.dot(normed, w_query, preferred_element_type=jnp.float32),
            jnp.dot(normed, w_key, preferred_element_type=jnp.float32),
            jnp.dot(normed, w_value, preferred_element_type=jnp.float32),
        ],
        axis=1,
    ).astype(jnp.bfloat16)
    outgate = jnp.dot(normed, w_outgate, preferred_element_type=jnp.float32)
    latent = jnp.dot(normed, gate_down, preferred_element_type=jnp.float32)
    logits = jnp.dot(latent, gate_up.astype(jnp.float32), precision=HIGHEST) + gate_bias
    log_decay = jax.nn.log_sigmoid(logits) / NORMALIZER
    previous = from_behind(projected[block_rows - (taps - 1) :], "seq", 1)
    extended = jnp.concatenate([previous, projected], axis=0)
    convolved = jax.nn.silu(short_conv(extended, segment_ext, conv_weight, block_rows)).astype(
        jnp.bfloat16
    )
    key_total = w_query.shape[1]
    value_total = w_value.shape[1]
    key_width = key_total // HEADS
    value_width = value_total // HEADS
    query = convolved[:, :key_total].astype(jnp.float32)
    keys = convolved[:, key_total : 2 * key_total].astype(jnp.float32)
    values = convolved[:, 2 * key_total :].reshape(block_rows, HEADS, value_width)

    order = jnp.arange(block_rows)
    lower = (order[:, None] >= order[None, :]).astype(jnp.float32)
    cumulative = jnp.dot(lower, log_decay, precision=HIGHEST)
    tail = cumulative[-1]
    keep = (segment == segment[-1]).astype(jnp.float32)
    keys_left = (keys * jnp.exp(tail[None] - cumulative) * keep[:, None]).reshape(
        block_rows, HEADS, key_width
    )
    state = jnp.einsum(
        "uhk,uhv->hkv", keys_left, values.astype(jnp.float32), precision=HIGHEST
    )
    decay = jnp.exp(tail) * (segment[-1] == segment_before).astype(jnp.float32)
    piece = key_total // devices
    pieces = state.astype(jnp.bfloat16).reshape(devices, piece, value_width)
    arrived = lax.all_to_all(pieces, "seq", split_axis=0, concat_axis=0, tiled=True)
    decays = lax.all_gather(decay, "seq").reshape(devices, devices, piece)
    mine = jnp.sum(
        jnp.where((jnp.arange(devices) == slice_index)[None, :, None], decays, 0.0), axis=1
    )
    before = [jnp.zeros((piece, value_width), jnp.float32)]
    for source in range(devices - 1):
        before.append(before[-1] * mine[source][:, None] + arrived[source].astype(jnp.float32))
    returned = lax.all_to_all(
        jnp.stack(before).astype(jnp.bfloat16), "seq", split_axis=0, concat_axis=0, tiled=True
    )
    incoming = returned.reshape(HEADS, key_width, value_width)

    allowed = (segment[:, None] == segment[None, :]) & (order[:, None] >= order[None, :])
    gap = jnp.where(allowed[:, :, None], cumulative[:, None] - cumulative[None, :], 0.0)
    products = query[:, None] * keys[None, :] * jnp.exp(gap)
    scores = jnp.sum(products.reshape(block_rows, block_rows, HEADS, key_width), axis=-1)
    scores = (scores * allowed[:, :, None].astype(jnp.float32)).astype(jnp.bfloat16)
    inner = jnp.einsum("tsh,shv->thv", scores, values, preferred_element_type=jnp.float32)
    clean = (segment == segment_before).astype(jnp.float32)
    query_decayed = (query * jnp.exp(cumulative) * clean[:, None]).reshape(
        block_rows, HEADS, key_width
    )
    carried = jnp.einsum(
        "thk,hkv->thv", query_decayed, incoming.astype(jnp.float32), precision=HIGHEST
    )
    attended = inner + carried
    gated = rms_scale(attended, head_gain.astype(jnp.float32)).reshape(
        block_rows, value_total
    ) * jax.nn.silu(outgate)
    resident = (
        jnp.dot(gated.astype(jnp.bfloat16), w_out, preferred_element_type=jnp.float32)
        + inputs.astype(jnp.float32)
    ).astype(jnp.bfloat16)

    mlp_normed = rms_scale(
        resident.astype(jnp.float32), forward_norm_scale.astype(jnp.float32)
    ).astype(jnp.bfloat16)
    swap = [(device, device ^ 1) for device in range(devices)]
    both_rows = jnp.concatenate([mlp_normed, lax.ppermute(mlp_normed, "seq", swap)], axis=0)
    width = inputs.shape[1]
    total = jnp.zeros((2 * block_rows, width), jnp.float32)
    gate_all, up_all, down_all = [
        full.reshape(SIDE, width, HALF) for full in (gate_all, up_all, down_all)
    ]
    for quarter in range(SIDE):
        gate = jnp.dot(both_rows, gate_all[quarter], preferred_element_type=jnp.float32)
        upward = jnp.dot(both_rows, up_all[quarter], preferred_element_type=jnp.float32)
        hidden = (jax.nn.silu(gate) * upward).astype(jnp.bfloat16)
        total = total + lax.dot_general(
            hidden, down_all[quarter], (((1,), (1,)), ((), ())), preferred_element_type=jnp.float32
        )
    other = lax.ppermute(total[block_rows:].astype(jnp.bfloat16), "seq", swap)
    mlp_own = (total[:block_rows] + other.astype(jnp.float32)).astype(jnp.bfloat16)
    output = jnp.where(
        valid[:, None], resident.astype(jnp.float32) + mlp_own.astype(jnp.float32), 0.0
    ).astype(jnp.bfloat16)
    return output[None]


def solution(mesh):
    return jax.shard_map(
        shards,
        mesh=mesh,
        in_specs=(P("req", "seq", None),) + (P(),) * 13 + (P("seq", "req"),) * 3,
        out_specs=P("req", "seq", None),
        check_vma=False,
    )
```

```python
import jax
import jax.numpy as jnp
from jax import lax
from jax.experimental import pallas as pl
from jax.experimental.pallas import tpu as pltpu
from jax.sharding import PartitionSpec as P

HEADS = 2
EPSILON = 1e-05
NORMALIZER = 16.0
HIGHEST = lax.Precision.HIGHEST
MESH = pl.DeviceIdType.MESH
F32 = jnp.float32
BF16 = jnp.bfloat16

SIDE = 4
BLOCKS = SIDE**3
DEVICES = 2 * SIDE * SIDE
HALF = 384
ROWS = 128
SUB = 16
HALO = 16
WIDTH = 2048
KEYS = 512
VALUES = 1024
KW = KEYS // HEADS
VW = VALUES // HEADS
PIECE = KEYS // DEVICES
ORDERS = (("x", "y", "z"), ("z", "x", "y"), ("y", "z", "x"))
KEEP, CLEAN, VALID = 4, 5, 6


def place():
    seq = lax.axis_index("seq")
    return {
        "x": seq // (2 * SIDE),
        "z": (seq // 2) % SIDE,
        "y": lax.axis_index("req"),
        "c": seq % 2,
    }


def device_at(at):
    return (at["y"], (at["x"] * SIDE + at["z"]) * 2 + at["c"])


def moved(at, axis, by):
    new = dict(at)
    new[axis] = (at[axis] + by + SIDE) % SIDE
    return new


def dot(a, b):
    return jnp.dot(a, b, preferred_element_type=F32)


def dot_nt(a, b):
    return lax.dot_general(a, b, (((1,), (1,)), ((), ())), preferred_element_type=F32)


def split(a):
    high = a.astype(BF16)
    return high, (a - high.astype(F32)).astype(BF16)


def silu(a):
    return a * jax.nn.sigmoid(a)


def layer_kernel(
    tokens,
    attn_gain,
    gate_down,
    gate_up,
    gate_bias,
    conv_weight,
    head_gain,
    forward_scale,
    masks,
    allowed,
    w_query,
    w_key,
    w_value,
    w_outgate,
    w_out_hbm,
    gate_shard,
    up_shard,
    down_shard,
    out,
    wg,
    wu,
    wd,
    staged,
    w_attn,
    w_out,
    normed,
    proj,
    outgate,
    query,
    keys,
    values,
    total,
    state_out,
    decay_out,
    state_in,
    decay_in,
    before,
    incoming,
    scores,
    gated,
    resident,
    x_rows,
    hidden,
    acc,
    other_send,
    other_recv,
    load_sem,
    local_sem,
    pair_send,
    pair_recv,
    send_sem,
    recv_sem,
    halo_sem,
    state_sem,
    swap_sem,
):
    me = place()
    core = me["c"]
    seq = lax.axis_index("seq")
    req = lax.axis_index("req")
    sibling = dict(me, c=1 - core)
    onward = 1 - 2 * core

    loads = []
    for index, (source, first, count) in enumerate(
        (
            (w_query, 0, KEYS),
            (w_key, KEYS, KEYS),
            (w_value, 2 * KEYS, VALUES),
            (w_outgate, 2 * KEYS + VALUES, VALUES),
        )
    ):
        load = pltpu.make_async_copy(
            source, w_attn.at[:, pl.ds(first, count)], load_sem.at[index]
        )
        load.start()
        loads.append(load)
    load_out = pltpu.make_async_copy(w_out_hbm, w_out, load_sem.at[4])
    load_out.start()

    barrier = pltpu.get_barrier_semaphore()

    def greet(step, carry):
        pl.semaphore_signal(
            barrier, inc=1, device_id=(req, (seq + step) % DEVICES), device_id_type=MESH
        )
        return carry

    lax.fori_loop(1, DEVICES, greet, 0)
    for by in (1, -1):
        pl.semaphore_signal(
            barrier, inc=1, device_id=device_at(moved(me, "y", by)), device_id_type=MESH
        )
    pl.semaphore_wait(barrier, DEVICES + 1)

    def slot(part, at):
        column = at["x"] * SIDE + at["z"]
        if part == 2:
            return wd.at[
                pl.ds(pl.multiple_of(at["y"] * HALF, 128), HALF),
                pl.ds(pl.multiple_of(column * 128, 128), 128),
            ]
        block = at["y"] * (SIDE * SIDE) + column
        return (wg, wu)[part].at[pl.ds(pl.multiple_of(block * 128, 128), 128), :]

    def own_half(part, source_core):
        if part == 2:
            return staged.at[pl.ds(pl.multiple_of(source_core * 64, 64), 64), :]
        block = (me["y"] * SIDE + me["x"]) * SIDE + me["z"]
        first = pl.multiple_of(block * 128 + source_core * 64, 64)
        return (wg, wu)[part].at[pl.ds(first, 64), :]

    locals_, pairs = [], []
    for part, shard in enumerate((gate_shard, up_shard, down_shard)):
        pair = pltpu.make_async_remote_copy(
            src_ref=shard.at[:, pl.ds(pl.multiple_of((1 - core) * HALF, 128), HALF)],
            dst_ref=own_half(part, core),
            send_sem=pair_send.at[part],
            recv_sem=pair_recv.at[part],
            device_id=device_at(sibling),
            device_id_type=MESH,
        )
        pair.start()
        pairs.append(pair)
        own = pltpu.make_async_copy(
            shard.at[:, pl.ds(pl.multiple_of(core * HALF, 128), HALF)],
            own_half(part, core),
            local_sem.at[part],
        )
        own.start()
        locals_.append(own)

    def block_of(at):
        return (at["y"] * SIDE + at["x"]) * SIDE + at["z"]

    def copy_of(part, at, axis, by):
        return pltpu.make_async_remote_copy(
            src_ref=slot(part, at),
            dst_ref=slot(part, at),
            send_sem=send_sem.at[part],
            recv_sem=recv_sem.at[part, block_of(at)],
            device_id=device_at(moved(me, axis, by)),
            device_id_type=MESH,
        )

    def send(part, at, axis, by):
        copy_of(part, at, axis, by).start()

    def both(part, at, axis):
        send(part, at, axis, 1)
        send(part, at, axis, -1)

    def arrive(part, at):
        copy_of(part, at, "x", 1).wait_recv()

    kinds = (-onward, onward, 2)

    def at_of(part, *steps):
        at = dict(me)
        for axis, by in zip(ORDERS[part], steps):
            at[axis] = (me[axis] + by + SIDE) % SIDE
        return at

    def first_axis(kind):
        for part in range(3):
            at = at_of(part, kinds[kind])
            arrive(part, at)
            if kind == 0:
                send(part, at, ORDERS[part][0], onward)
            both(part, at, ORDERS[part][1])
            both(part, at, ORDERS[part][2])

    def second_axis(kind):
        def step_(step, carry):
            for part in range(3):
                at = at_of(part, step, kinds[kind])
                arrive(part, at)
                if kind == 0:
                    send(part, at, ORDERS[part][1], onward)
                both(part, at, ORDERS[part][2])
            return carry

        lax.fori_loop(0, SIDE, step_, 0)

    def third_axis(kind, second, parts=(0, 1, 2)):
        def step_(step, carry):
            for part in parts:
                at = at_of(part, step, second, kinds[kind])
                arrive(part, at)
                if kind == 0:
                    send(part, at, ORDERS[part][2], onward)
            return carry

        lax.fori_loop(0, SIDE, step_, 0)

    inputs = tokens[...].astype(F32)
    mean_square = jnp.mean(inputs * inputs, axis=-1, keepdims=True)
    normed[...] = (
        inputs * lax.rsqrt(mean_square + EPSILON) * attn_gain[...].astype(F32)
    ).astype(BF16)

    for part in range(3):
        locals_[part].wait()
        pairs[part].wait_recv()
        if part == 2:
            ref = slot(2, me)
            ref[...] = jnp.transpose(staged[...].astype(F32)).astype(BF16)
        both(part, me, ORDERS[part][0])
    for part in range(3):
        both(part, me, ORDERS[part][1])
    for part in range(3):
        both(part, me, ORDERS[part][2])

    def project(index, carry):
        columns = pl.ds(pl.multiple_of(index * 256, 256), 256)
        proj[pl.ds(HALO, ROWS), columns] = dot(normed[...], w_attn[:, columns]).astype(BF16)
        return carry

    loads[0].wait()
    loads[1].wait()
    lax.fori_loop(0, 4, project, 0)
    loads[2].wait()
    lax.fori_loop(4, 8, project, 0)
    halo = pltpu.make_async_remote_copy(
        src_ref=proj.at[pl.ds(ROWS, HALO), :],
        dst_ref=proj.at[pl.ds(0, HALO), :],
        send_sem=halo_sem.at[0],
        recv_sem=halo_sem.at[1],
        device_id=(req, (seq + 1) % DEVICES),
        device_id_type=MESH,
    )
    halo.start()

    for kind in range(3):
        first_axis(kind)

    def project_gate(index, carry):
        source = pl.ds(pl.multiple_of(index * 256 + 2 * KEYS + VALUES, 256), 256)
        target = pl.ds(pl.multiple_of(index * 256, 256), 256)
        outgate[:, target] = dot(normed[...], w_attn[:, source])
        return carry

    loads[3].wait()
    lax.fori_loop(0, 4, project_gate, 0)
    latent = dot(normed[...], gate_down[...])
    logits = (
        jnp.dot(latent, gate_up[...].astype(F32), precision=HIGHEST, preferred_element_type=F32)
        + gate_bias[...]
    )
    log_decay = (jnp.minimum(logits, 0.0) - jnp.log1p(jnp.exp(-jnp.abs(logits)))) / NORMALIZER
    row = lax.broadcasted_iota(jnp.int32, (ROWS, ROWS), 0)
    lane = lax.broadcasted_iota(jnp.int32, (ROWS, ROWS), 1)
    lower = (row >= lane).astype(F32)
    cumulative = jnp.dot(lower, log_decay, precision=HIGHEST, preferred_element_type=F32)
    total[...] = cumulative.reshape(ROWS // SUB, SUB, KEYS)
    table = masks[...]
    clean_block = table[ROWS - 1 : ROWS, CLEAN : CLEAN + 1]
    tail_rows = jnp.dot(
        jnp.transpose(log_decay), jnp.ones((ROWS, 128), F32), precision=HIGHEST,
        preferred_element_type=F32,
    )
    decay_out[...] = jnp.exp(tail_rows) * clean_block

    halo.wait()
    for chunk in range(4):
        columns = slice(chunk * 512, (chunk + 1) * 512)
        rows = proj[:, columns].astype(F32)
        taps = conv_weight[:, columns].astype(F32)
        mixed = rows[HALO:] * taps[0:1]
        for tap in range(1, 4):
            shifted = pltpu.roll(rows, tap, 0)[HALO:]
            same = table[:, tap : tap + 1]
            mixed = mixed + taps[tap : tap + 1] * jnp.where(same > 0.0, shifted, 0.0)
        mixed = silu(mixed).astype(BF16)
        if chunk == 0:
            query[...] = mixed.astype(F32).reshape(ROWS // SUB, SUB, KEYS)
        elif chunk == 1:
            keys[...] = mixed.astype(F32).reshape(ROWS // SUB, SUB, KEYS)
        else:
            values[:, (chunk - 2) * 512 : (chunk - 1) * 512] = mixed

    tail = cumulative[ROWS - 1 : ROWS]
    keys_left = (
        keys[...].reshape(ROWS, KEYS) * jnp.exp(tail - cumulative) * table[:, KEEP : KEEP + 1]
    )
    for head in range(HEADS):
        high, low = split(jnp.transpose(keys_left[:, head * KW : (head + 1) * KW]))
        head_values = values[:, head * VW : (head + 1) * VW]
        state_out[head * KW : (head + 1) * KW, :] = (
            dot(high, head_values) + dot(low, head_values)
        ).astype(BF16)

    def piece_of(ref, index):
        return ref.at[pl.ds(pl.multiple_of(index * PIECE, PIECE), PIECE), :]

    def exchange(source, target, which):
        def step_(step, carry):
            to = (seq + step) % DEVICES
            pltpu.make_async_remote_copy(
                src_ref=piece_of(source, to),
                dst_ref=piece_of(target, seq),
                send_sem=state_sem.at[2 * which],
                recv_sem=state_sem.at[2 * which + 1],
                device_id=(req, to),
                device_id_type=MESH,
            ).start()
            return carry

        lax.fori_loop(1, DEVICES, step_, 0)

    def exchanged(source, target, which):
        count = (DEVICES - 1) * PIECE
        return pltpu.make_async_remote_copy(
            src_ref=source.at[pl.ds(0, count), :],
            dst_ref=target.at[pl.ds(0, count), :],
            send_sem=state_sem.at[2 * which],
            recv_sem=state_sem.at[2 * which + 1],
            device_id=device_at(sibling),
            device_id_type=MESH,
        )

    exchange(decay_out, decay_in, 0)
    exchange(state_out, state_in, 1)
    mine = pl.ds(pl.multiple_of(seq * PIECE, PIECE), PIECE)
    decay_in[mine, :] = decay_out[mine, :]
    state_in[mine, :] = state_out[mine, :]

    second_axis(0)

    scores[...] = jnp.zeros_like(scores)
    sub_row = row // SUB

    def diagonal(step, carry):
        key_row = keys[:, pl.ds(step, 1), :]
        total_row = total[:, pl.ds(step, 1), :]
        product = query[...] * key_row * jnp.exp(jnp.minimum(total[...] - total_row, 0.0))
        here = lane == sub_row * SUB + step
        for head in range(HEADS):
            summed = jnp.sum(product[:, :, head * KW : (head + 1) * KW], axis=-1, keepdims=True)
            scores[head] += jnp.where(here, summed.reshape(ROWS, 1), 0.0)
        return carry

    lax.fori_loop(0, SUB, diagonal, 0)
    flat_keys = keys[...].reshape(ROWS, KEYS)
    for sub in range(1, ROWS // SUB):
        base = total[sub - 1, SUB - 1 : SUB, :]
        query_high, query_low = split(query[sub] * jnp.exp(total[sub] - base))
        key_high, key_low = split(flat_keys * jnp.exp(jnp.minimum(base - cumulative, 0.0)))
        for head in range(HEADS):
            part = slice(head * KW, (head + 1) * KW)
            block = (
                dot_nt(query_high[:, part], key_high[:, part])
                + dot_nt(query_high[:, part], key_low[:, part])
                + dot_nt(query_low[:, part], key_high[:, part])
            )
            rows = slice(sub * SUB, (sub + 1) * SUB)
            scores[head, rows, :] += jnp.where(lane[:SUB] < sub * SUB, block, 0.0)

    exchanged(decay_out, decay_in, 0).wait_recv()
    exchanged(state_out, state_in, 1).wait_recv()

    def prefix(step, running):
        rows = pl.ds(pl.multiple_of(step * PIECE, PIECE), PIECE)
        before[rows, :] = running.astype(BF16)
        decay = decay_in[rows, :]
        decay = jnp.concatenate([decay] * (VW // 128), axis=1)
        return running * decay + state_in[rows, :].astype(F32)

    lax.fori_loop(0, DEVICES, prefix, jnp.zeros((PIECE, VW), F32))
    exchange(before, incoming, 2)
    incoming[mine, :] = before[mine, :]

    second_axis(1)
    second_axis(2)
    third_axis(0, 0)

    exchanged(before, incoming, 2).wait_recv()
    query_decayed = (
        query[...].reshape(ROWS, KEYS) * jnp.exp(cumulative) * table[:, CLEAN : CLEAN + 1]
    )
    for head in range(HEADS):
        key_part = slice(head * KW, (head + 1) * KW)
        value_part = slice(head * VW, (head + 1) * VW)
        high, low = split(query_decayed[:, key_part])
        weights = (scores[head] * allowed[...]).astype(BF16)
        before_state = incoming[key_part, :]
        attended = (
            dot(weights, values[:, value_part]) + dot(high, before_state) + dot(low, before_state)
        )
        mean_square = jnp.mean(attended * attended, axis=-1, keepdims=True)
        scaled = attended * lax.rsqrt(mean_square + EPSILON) * head_gain[...].astype(F32)
        gated[:, value_part] = (scaled * silu(outgate[:, value_part])).astype(BF16)

    load_out.wait()

    def project_out(index, carry):
        columns = pl.ds(pl.multiple_of(index * 256, 256), 256)
        resident[:, columns] = (
            dot(gated[...], w_out[:, columns]) + tokens[:, columns].astype(F32)
        ).astype(BF16)
        return carry

    lax.fori_loop(0, WIDTH // 256, project_out, 0)
    wide = resident[...].astype(F32)
    mean_square = jnp.mean(wide * wide, axis=-1, keepdims=True)
    own_rows = pl.ds(pl.multiple_of(core * ROWS, ROWS), ROWS)
    other_rows = pl.ds(pl.multiple_of((1 - core) * ROWS, ROWS), ROWS)
    x_rows[own_rows, :] = (
        wide * lax.rsqrt(mean_square + EPSILON) * forward_scale[...].astype(F32)
    ).astype(BF16)
    swap_x = pltpu.make_async_remote_copy(
        src_ref=x_rows.at[own_rows, :],
        dst_ref=x_rows.at[own_rows, :],
        send_sem=swap_sem.at[0],
        recv_sem=swap_sem.at[1],
        device_id=device_at(sibling),
        device_id_type=MESH,
    )
    swap_x.start()

    for second in kinds:
        third_axis(0, second)
    for second in (0,) + kinds:
        third_axis(1, second)
        third_axis(2, second)
    swap_x.wait()

    for quarter in range(SIDE):
        columns = slice(quarter * HALF, (quarter + 1) * HALF)
        features = slice(quarter * WIDTH, (quarter + 1) * WIDTH)
        gate = dot(x_rows[...], wg[features, :])
        upward = dot(x_rows[...], wu[features, :])
        hidden[:, columns] = (silu(gate) * upward).astype(BF16)

    def project_down(index, carry):
        columns = pl.ds(pl.multiple_of(index * 256, 256), 256)
        acc[:, columns] = dot(hidden[...], wd[:, columns])
        return carry

    lax.fori_loop(0, WIDTH // 256, project_down, 0)
    other_send[...] = acc[other_rows, :].astype(BF16)
    swap_out = pltpu.make_async_remote_copy(
        src_ref=other_send,
        dst_ref=other_recv,
        send_sem=swap_sem.at[2],
        recv_sem=swap_sem.at[3],
        device_id=device_at(sibling),
        device_id_type=MESH,
    )
    swap_out.start()
    swap_out.wait()
    mlp = (acc[own_rows, :] + other_recv[...].astype(F32)).astype(BF16)
    result = resident[...].astype(F32) + mlp.astype(F32)
    out[...] = jnp.where(table[:, VALID : VALID + 1] > 0.0, result, 0.0).astype(BF16)

    exchanged(decay_out, decay_in, 0).wait_send()
    exchanged(state_out, state_in, 1).wait_send()
    exchanged(before, incoming, 2).wait_send()
    for part in range(3):
        pairs[part].wait_send()
        sent = wg.at[pl.ds(0, (BLOCKS - 1) * 128), :]
        pltpu.make_async_remote_copy(
            src_ref=sent,
            dst_ref=sent,
            send_sem=send_sem.at[part],
            recv_sem=recv_sem.at[part, 0],
            device_id=device_at(sibling),
            device_id_type=MESH,
        ).wait_send()


def layer(vmem_args, hbm_args):
    vmem = pl.BlockSpec(memory_space=pltpu.VMEM)
    hbm = pl.BlockSpec(memory_space=pl.ANY)
    dma = pltpu.SemaphoreType.DMA
    return pl.pallas_call(
        layer_kernel,
        out_shape=jax.ShapeDtypeStruct((ROWS, WIDTH), BF16),
        in_specs=[vmem] * len(vmem_args) + [hbm] * len(hbm_args),
        out_specs=vmem,
        scratch_shapes=[
            pltpu.VMEM((BLOCKS * 128, HALF), BF16),
            pltpu.VMEM((BLOCKS * 128, HALF), BF16),
            pltpu.VMEM((SIDE * HALF, WIDTH), BF16),
            pltpu.VMEM((128, HALF), BF16),
            pltpu.VMEM((WIDTH, 2 * KEYS + 2 * VALUES), BF16),
            pltpu.VMEM((VALUES, WIDTH), BF16),
            pltpu.VMEM((ROWS, WIDTH), BF16),
            pltpu.VMEM((HALO + ROWS, 2 * KEYS + VALUES), BF16),
            pltpu.VMEM((ROWS, VALUES), F32),
            pltpu.VMEM((ROWS // SUB, SUB, KEYS), F32),
            pltpu.VMEM((ROWS // SUB, SUB, KEYS), F32),
            pltpu.VMEM((ROWS, VALUES), BF16),
            pltpu.VMEM((ROWS // SUB, SUB, KEYS), F32),
            pltpu.VMEM((KEYS, VW), BF16),
            pltpu.VMEM((KEYS, 128), F32),
            pltpu.VMEM((KEYS, VW), BF16),
            pltpu.VMEM((KEYS, 128), F32),
            pltpu.VMEM((KEYS, VW), BF16),
            pltpu.VMEM((KEYS, VW), BF16),
            pltpu.VMEM((HEADS, ROWS, ROWS), F32),
            pltpu.VMEM((ROWS, VALUES), BF16),
            pltpu.VMEM((ROWS, WIDTH), BF16),
            pltpu.VMEM((2 * ROWS, WIDTH), BF16),
            pltpu.VMEM((2 * ROWS, SIDE * HALF), BF16),
            pltpu.VMEM((2 * ROWS, WIDTH), F32),
            pltpu.VMEM((ROWS, WIDTH), BF16),
            pltpu.VMEM((ROWS, WIDTH), BF16),
            dma((5,)),
            dma((3,)),
            dma((3,)),
            dma((3,)),
            dma((3,)),
            dma((3, BLOCKS)),
            dma((2,)),
            dma((6,)),
            dma((4,)),
        ],
        compiler_params=pltpu.CompilerParams(
            collective_id=0, has_side_effects=True, vmem_limit_bytes=67043328
        ),
        name="layer",
    )(*vmem_args, *hbm_args)


def segment_ids(positions, bounds):
    return jnp.sum((positions[:, None] >= bounds[None, :]).astype(jnp.int32), axis=1)


def shards(
    tokens,
    lengths,
    attn_gain,
    w_query,
    w_key,
    w_value,
    w_outgate,
    gate_down,
    gate_up,
    gate_bias,
    conv_weight,
    head_gain,
    w_out,
    forward_norm_scale,
    w_gate,
    w_up,
    down_weight,
):
    group_index = lax.axis_index("req")
    slice_index = lax.axis_index("seq")
    request_slots = lengths.shape[1]
    bounds_all = jnp.cumsum(lengths, axis=1)
    group_row = jnp.arange(lengths.shape[0], dtype=jnp.int32) == group_index
    bounds = jnp.sum(jnp.where(group_row[:, None], bounds_all, 0), axis=0)
    positions = slice_index * ROWS - 3 + jnp.arange(ROWS + 3, dtype=jnp.int32)
    segment_ext = jnp.where(positions < 0, -1, segment_ids(positions, bounds))
    segment = segment_ext[3:]
    columns = [segment >= 0]
    columns += [segment_ext[3 - tap : 3 - tap + ROWS] == segment for tap in (1, 2, 3)]
    columns += [segment == segment[-1], segment == segment_ext[2], segment < request_slots]
    masks = jnp.stack(columns, axis=1).astype(F32)
    masks = jnp.pad(masks, ((0, 0), (0, 128 - masks.shape[1])))
    order = jnp.arange(ROWS)
    allowed = (segment[:, None] == segment[None, :]) & (order[:, None] >= order[None, :])
    padded = [
        jnp.pad(shard, ((0, 0), (0, 2 * HALF - shard.shape[1])))
        for shard in (w_gate, w_up, down_weight)
    ]
    output = layer(
        (
            tokens[0],
            attn_gain[None],
            gate_down,
            gate_up,
            gate_bias[None],
            conv_weight,
            head_gain[None],
            forward_norm_scale[None],
            masks,
            allowed.astype(F32),
        ),
        (w_query, w_key, w_value, w_outgate, w_out, *padded),
    )
    return output[None]


def solution(mesh):
    return jax.shard_map(
        shards,
        mesh=mesh,
        in_specs=(P("req", "seq", None),) + (P(),) * 13 + (P("seq", "req"),) * 3,
        out_specs=P("req", "seq", None),
        check_vma=False,
    )
```

```python
import jax
import jax.numpy as jnp
from jax import lax
from jax.experimental import pallas as pl
from jax.experimental.pallas import tpu as pltpu
from jax.sharding import PartitionSpec as P

HEADS = 2
EPSILON = 1e-05
NORMALIZER = 16.0
HIGHEST = lax.Precision.HIGHEST
MESH = pl.DeviceIdType.MESH
F32 = jnp.float32
BF16 = jnp.bfloat16

SIDE = 4
BLOCKS = SIDE**3
DEVICES = 2 * SIDE * SIDE
HALF = 352
WIDE = 384
QUARTER = 2 * HALF
ROWS = 128
SUB = 16
HALO = 16
WIDTH = 2048
KEYS = 512
VALUES = 1024
KW = KEYS // HEADS
VW = VALUES // HEADS
PIECE = KEYS // DEVICES
REQUESTS = 4
VMEM_LIMIT = 56 * 2**20
ORDERS = (("x", "y", "z"), ("z", "x", "y"), ("y", "z", "x"))


def place():
    seq = lax.axis_index("seq")
    return {
        "x": seq // (2 * SIDE),
        "z": (seq // 2) % SIDE,
        "y": lax.axis_index("req"),
        "c": seq % 2,
    }


def device_at(at):
    return (at["y"], (at["x"] * SIDE + at["z"]) * 2 + at["c"])


def moved(at, axis, by):
    new = dict(at)
    new[axis] = (at[axis] + by + SIDE) % SIDE
    return new


def dot(a, b):
    return jnp.dot(a, b, preferred_element_type=F32)


def dot_nt(a, b):
    return lax.dot_general(a, b, (((1,), (1,)), ((), ())), preferred_element_type=F32)


def split(a):
    high = a.astype(BF16)
    return high, (a - high.astype(F32)).astype(BF16)


def silu(a):
    return a * jax.nn.sigmoid(a)


def layer_kernel(
    lengths,
    tokens,
    vectors,
    gate_down,
    gate_up,
    conv_weight,
    gate_shard,
    up_shard,
    down_shard,
    w_query,
    w_key,
    w_value,
    w_outgate,
    w_out_hbm,
    out,
    wg,
    wu,
    wd,
    turned,
    pair_in,
    w_attn,
    w_out,
    normed,
    proj,
    outgate,
    query,
    keys,
    values,
    total,
    state_out,
    decay_out,
    state_in,
    decay_in,
    before,
    incoming,
    scores,
    gated,
    resident,
    x_rows,
    hidden,
    acc,
    other_send,
    other_recv,
    load_sem,
    pair_send,
    pair_recv,
    send_sem,
    recv_sem,
    halo_sem,
    state_sem,
    swap_sem,
    out_sem,
):
    me = place()
    core = me["c"]
    seq = lax.axis_index("seq")
    req = lax.axis_index("req")
    sibling = dict(me, c=1 - core)
    onward = 1 - 2 * core

    loads = []
    for index, (source, first, count) in enumerate(
        (
            (w_query, 0, KEYS),
            (w_key, KEYS, KEYS),
            (w_value, 2 * KEYS, VALUES),
            (w_outgate, 2 * KEYS + VALUES, VALUES),
        )
    ):
        load = pltpu.make_async_copy(
            source, w_attn.at[:, pl.ds(first, count)], load_sem.at[index]
        )
        load.start()
        loads.append(load)
    load_out = pltpu.make_async_copy(w_out_hbm, w_out, load_sem.at[4])
    load_out.start()

    barrier = pltpu.get_barrier_semaphore()

    def greet(step, carry):
        pl.semaphore_signal(
            barrier, inc=1, device_id=(req, (seq + step) % DEVICES), device_id_type=MESH
        )
        return carry

    lax.fori_loop(1, DEVICES, greet, 0)
    for by in (1, -1):
        pl.semaphore_signal(
            barrier, inc=1, device_id=device_at(moved(me, "y", by)), device_id_type=MESH
        )
    for part, shard in enumerate((gate_shard, up_shard, down_shard)):
        columns = jnp.transpose(shard[...].astype(F32))
        zeros = jnp.zeros_like(columns)
        turned[part] = jnp.where(
            core == 0,
            jnp.concatenate([columns, zeros], axis=1),
            jnp.concatenate([zeros, columns], axis=1),
        ).astype(BF16)
    for quarter in range(SIDE):
        wd[:, quarter * WIDE + HALF : (quarter + 1) * WIDE, :] = jnp.zeros(
            (SIDE * SIDE, WIDE - HALF, 128), BF16
        )
    pl.semaphore_wait(barrier, DEVICES + 1)

    fulls = (wg, wu, wd)
    strides = (HALF, HALF, WIDE)

    def slot(part, at):
        first = pl.multiple_of(at["y"] * strides[part], 32)
        return fulls[part].at[at["x"] * SIDE + at["z"], pl.ds(first, HALF), :]

    pairs = []
    for part in range(3):
        pair = pltpu.make_async_remote_copy(
            src_ref=turned.at[part, pl.ds(pl.multiple_of((1 - core) * HALF, 32), HALF), :],
            dst_ref=pair_in.at[part],
            send_sem=pair_send.at[part],
            recv_sem=pair_recv.at[part],
            device_id=device_at(sibling),
            device_id_type=MESH,
        )
        pair.start()
        pairs.append(pair)

    def block_of(at):
        return (at["y"] * SIDE + at["x"]) * SIDE + at["z"]

    def copy_of(part, at, axis, by):
        return pltpu.make_async_remote_copy(
            src_ref=slot(part, at),
            dst_ref=slot(part, at),
            send_sem=send_sem.at[part],
            recv_sem=recv_sem.at[part, block_of(at)],
            device_id=device_at(moved(me, axis, by)),
            device_id_type=MESH,
        )

    def send(part, at, axis, by):
        copy_of(part, at, axis, by).start()

    def both(part, at, axis):
        send(part, at, axis, 1)
        send(part, at, axis, -1)

    def arrive(part, at):
        copy_of(part, at, "x", 1).wait_recv()

    kinds = (-onward, onward, 2)

    def at_of(part, *steps):
        at = dict(me)
        for axis, by in zip(ORDERS[part], steps):
            at[axis] = (me[axis] + by + SIDE) % SIDE
        return at

    def first_axis(kind):
        for part in range(3):
            at = at_of(part, kinds[kind])
            arrive(part, at)
            if kind == 0:
                send(part, at, ORDERS[part][0], onward)
            both(part, at, ORDERS[part][1])
            both(part, at, ORDERS[part][2])

    def offset(step):
        side = jnp.where(step == 1, -onward, onward)
        return jnp.where(step == 0, 0, jnp.where(step == 3, 2, side))

    def second_axis(kind):
        def step_(step, carry):
            for part in range(3):
                at = at_of(part, offset(step), kinds[kind])
                arrive(part, at)
                if kind == 0:
                    send(part, at, ORDERS[part][1], onward)
                both(part, at, ORDERS[part][2])
            return carry

        lax.fori_loop(0, SIDE, step_, 0)

    def third_axis(kind, second, parts=(0, 1, 2)):
        def step_(step, carry):
            for part in parts:
                at = at_of(part, offset(step), second, kinds[kind])
                arrive(part, at)
                if kind == 0:
                    send(part, at, ORDERS[part][2], onward)
            return carry

        lax.fori_loop(0, SIDE, step_, 0)

    inputs = tokens[...].astype(F32)
    mean_square = jnp.mean(inputs * inputs, axis=-1, keepdims=True)
    normed[...] = (
        inputs * lax.rsqrt(mean_square + EPSILON) * vectors[0:1, :]
    ).astype(BF16)

    for part in range(3):
        pairs[part].wait_recv()
        own = turned[part, pl.ds(pl.multiple_of(core * HALF, 32), HALF), :]
        block = slot(part, me)
        block[...] = own + pair_in[part]
        both(part, me, ORDERS[part][0])
    for part in range(3):
        both(part, me, ORDERS[part][1])
    for part in range(3):
        both(part, me, ORDERS[part][2])

    def project(index, carry):
        columns = pl.ds(pl.multiple_of(index * 256, 256), 256)
        proj[pl.ds(HALO, ROWS), columns] = dot(normed[...], w_attn[:, columns]).astype(BF16)
        return carry

    loads[0].wait()
    loads[1].wait()
    lax.fori_loop(0, 4, project, 0)
    loads[2].wait()
    lax.fori_loop(4, 8, project, 0)
    halo = pltpu.make_async_remote_copy(
        src_ref=proj.at[pl.ds(ROWS, HALO), :],
        dst_ref=proj.at[pl.ds(0, HALO), :],
        send_sem=halo_sem.at[0],
        recv_sem=halo_sem.at[1],
        device_id=(req, (seq + 1) % DEVICES),
        device_id_type=MESH,
    )
    halo.start()

    for kind in range(3):
        first_axis(kind)

    def project_gate(index, carry):
        source = pl.ds(pl.multiple_of(index * 256 + 2 * KEYS + VALUES, 256), 256)
        target = pl.ds(pl.multiple_of(index * 256, 256), 256)
        outgate[:, target] = dot(normed[...], w_attn[:, source])
        return carry

    loads[3].wait()
    lax.fori_loop(0, 4, project_gate, 0)
    latent = dot_nt(normed[...], gate_down[...])
    logits = (
        jnp.dot(latent, gate_up[...].astype(F32), precision=HIGHEST, preferred_element_type=F32)
        + vectors[2:3, 0:KEYS]
    )
    log_decay = (jnp.minimum(logits, 0.0) - jnp.log1p(jnp.exp(-jnp.abs(logits)))) / NORMALIZER
    row = lax.broadcasted_iota(jnp.int32, (ROWS, ROWS), 0)
    lane = lax.broadcasted_iota(jnp.int32, (ROWS, ROWS), 1)
    lower = (row >= lane).astype(F32)
    cumulative = jnp.dot(lower, log_decay, precision=HIGHEST, preferred_element_type=F32)
    total[...] = cumulative.reshape(ROWS // SUB, SUB, KEYS)
    bounds = [lengths[req, 0]]
    for slot_index in range(1, REQUESTS):
        bounds.append(bounds[-1] + lengths[req, slot_index])

    def segment_of(position):
        count = jnp.zeros_like(position)
        for bound in bounds:
            count = count + (position >= bound).astype(jnp.int32)
        return jnp.where(position < 0, -1, count)

    def column_mask(same):
        return same.astype(F32)[:, :1]

    position = seq * ROWS + row
    segment = segment_of(position)
    allowed = ((segment == segment_of(seq * ROWS + lane)) & (row >= lane)).astype(F32)
    taps_same = [None] + [column_mask(segment_of(position - tap) == segment) for tap in (1, 2, 3)]
    last_segment = segment_of(jnp.zeros_like(row) + (seq * ROWS + ROWS - 1))
    keep = column_mask(segment == last_segment)
    clean = column_mask(segment == segment_of(jnp.zeros_like(row) + (seq * ROWS - 1)))
    valid = column_mask(segment < REQUESTS)
    clean_block = clean[ROWS - 1 : ROWS]
    tail_rows = jnp.dot(
        jnp.transpose(log_decay), jnp.ones((ROWS, 128), F32), precision=HIGHEST,
        preferred_element_type=F32,
    )
    decay_out[...] = jnp.exp(tail_rows) * clean_block

    halo.wait()
    for chunk in range(4):
        columns = slice(chunk * 512, (chunk + 1) * 512)
        rows = proj[:, columns].astype(F32)
        taps = conv_weight[:, columns].astype(F32)
        mixed = rows[HALO:] * taps[0:1]
        for tap in range(1, 4):
            shifted = pltpu.roll(rows, tap, 0)[HALO:]
            mixed = mixed + taps[tap : tap + 1] * jnp.where(taps_same[tap] > 0.0, shifted, 0.0)
        mixed = silu(mixed).astype(BF16)
        if chunk == 0:
            query[...] = mixed.astype(F32).reshape(ROWS // SUB, SUB, KEYS)
        elif chunk == 1:
            keys[...] = mixed.astype(F32).reshape(ROWS // SUB, SUB, KEYS)
        else:
            values[:, (chunk - 2) * 512 : (chunk - 1) * 512] = mixed

    tail = cumulative[ROWS - 1 : ROWS]
    keys_left = (
        keys[...].reshape(ROWS, KEYS) * jnp.exp(tail - cumulative) * keep
    )
    for head in range(HEADS):
        high, low = split(jnp.transpose(keys_left[:, head * KW : (head + 1) * KW]))
        head_values = values[:, head * VW : (head + 1) * VW]
        state_out[head * KW : (head + 1) * KW, :] = (
            dot(high, head_values) + dot(low, head_values)
        ).astype(BF16)

    def piece_of(ref, index):
        return ref.at[pl.ds(pl.multiple_of(index * PIECE, PIECE), PIECE), :]

    def exchange(source, target, which):
        def step_(step, carry):
            to = (seq + step) % DEVICES
            pltpu.make_async_remote_copy(
                src_ref=piece_of(source, to),
                dst_ref=piece_of(target, seq),
                send_sem=state_sem.at[2 * which],
                recv_sem=state_sem.at[2 * which + 1],
                device_id=(req, to),
                device_id_type=MESH,
            ).start()
            return carry

        lax.fori_loop(1, DEVICES, step_, 0)

    def exchanged(source, target, which):
        count = (DEVICES - 1) * PIECE
        return pltpu.make_async_remote_copy(
            src_ref=source.at[pl.ds(0, count), :],
            dst_ref=target.at[pl.ds(0, count), :],
            send_sem=state_sem.at[2 * which],
            recv_sem=state_sem.at[2 * which + 1],
            device_id=device_at(sibling),
            device_id_type=MESH,
        )

    exchange(decay_out, decay_in, 0)
    exchange(state_out, state_in, 1)
    mine = pl.ds(pl.multiple_of(seq * PIECE, PIECE), PIECE)
    decay_in[mine, :] = decay_out[mine, :]
    state_in[mine, :] = state_out[mine, :]

    second_axis(0)

    scores[...] = jnp.zeros_like(scores)
    sub_row = row // SUB

    def diagonal(step, carry):
        key_row = keys[:, pl.ds(step, 1), :]
        total_row = total[:, pl.ds(step, 1), :]
        product = query[...] * key_row * jnp.exp(jnp.minimum(total[...] - total_row, 0.0))
        here = lane == sub_row * SUB + step
        for head in range(HEADS):
            summed = jnp.sum(product[:, :, head * KW : (head + 1) * KW], axis=-1, keepdims=True)
            scores[head] += jnp.where(here, summed.reshape(ROWS, 1), 0.0)
        return carry

    lax.fori_loop(0, SUB, diagonal, 0)
    flat_keys = keys[...].reshape(ROWS, KEYS)
    for sub in range(1, ROWS // SUB):
        base = total[sub - 1, SUB - 1 : SUB, :]
        query_high, query_low = split(query[sub] * jnp.exp(total[sub] - base))
        key_high, key_low = split(flat_keys * jnp.exp(jnp.minimum(base - cumulative, 0.0)))
        for head in range(HEADS):
            part = slice(head * KW, (head + 1) * KW)
            block = (
                dot_nt(query_high[:, part], key_high[:, part])
                + dot_nt(query_high[:, part], key_low[:, part])
                + dot_nt(query_low[:, part], key_high[:, part])
            )
            rows = slice(sub * SUB, (sub + 1) * SUB)
            scores[head, rows, :] += jnp.where(lane[:SUB] < sub * SUB, block, 0.0)

    exchanged(decay_out, decay_in, 0).wait_recv()
    exchanged(state_out, state_in, 1).wait_recv()

    def prefix(step, running):
        rows = pl.ds(pl.multiple_of(step * PIECE, PIECE), PIECE)
        before[rows, :] = running.astype(BF16)
        decay = decay_in[rows, :]
        decay = jnp.concatenate([decay] * (VW // 128), axis=1)
        return running * decay + state_in[rows, :].astype(F32)

    lax.fori_loop(0, DEVICES, prefix, jnp.zeros((PIECE, VW), F32))
    exchange(before, incoming, 2)
    incoming[mine, :] = before[mine, :]

    second_axis(1)
    second_axis(2)
    third_axis(0, 0)

    exchanged(before, incoming, 2).wait_recv()
    query_decayed = (
        query[...].reshape(ROWS, KEYS) * jnp.exp(cumulative) * clean
    )
    for head in range(HEADS):
        key_part = slice(head * KW, (head + 1) * KW)
        value_part = slice(head * VW, (head + 1) * VW)
        high, low = split(query_decayed[:, key_part])
        weights = (scores[head] * allowed).astype(BF16)
        before_state = incoming[key_part, :]
        attended = (
            dot(weights, values[:, value_part]) + dot(high, before_state) + dot(low, before_state)
        )
        mean_square = jnp.mean(attended * attended, axis=-1, keepdims=True)
        scaled = attended * lax.rsqrt(mean_square + EPSILON) * vectors[3:4, 0:VW]
        gated[:, value_part] = (scaled * silu(outgate[:, value_part])).astype(BF16)

    load_out.wait()

    def project_out(index, carry):
        columns = pl.ds(pl.multiple_of(index * 256, 256), 256)
        resident[:, columns] = (
            dot(gated[...], w_out[:, columns]) + tokens[:, columns].astype(F32)
        ).astype(BF16)
        return carry

    lax.fori_loop(0, WIDTH // 256, project_out, 0)
    wide = resident[...].astype(F32)
    mean_square = jnp.mean(wide * wide, axis=-1, keepdims=True)
    own_rows = pl.ds(pl.multiple_of(core * ROWS, ROWS), ROWS)
    other_rows = pl.ds(pl.multiple_of((1 - core) * ROWS, ROWS), ROWS)
    x_rows[:, own_rows] = jnp.transpose(
        wide * lax.rsqrt(mean_square + EPSILON) * vectors[1:2, :]
    ).astype(BF16)
    swap_x = pltpu.make_async_remote_copy(
        src_ref=x_rows.at[:, own_rows],
        dst_ref=x_rows.at[:, own_rows],
        send_sem=swap_sem.at[0],
        recv_sem=swap_sem.at[1],
        device_id=device_at(sibling),
        device_id_type=MESH,
    )
    swap_x.start()

    def swiglu(quarter):
        rows = pl.ds(pl.multiple_of(quarter * HALF, 32), HALF)

        def product(full):
            summed = None
            for index in range(WIDTH // 256):
                pair = jnp.concatenate([full[2 * index, rows, :], full[2 * index + 1, rows, :]], axis=1)
                term = dot(pair, x_rows[index * 256 : (index + 1) * 256, :])
                summed = term if summed is None else summed + term
            return summed

        units = silu(product(wg)) * product(wu)
        units = jnp.concatenate([units, jnp.zeros((WIDE - HALF, 2 * ROWS), F32)], axis=0)
        columns = pl.ds(pl.multiple_of(quarter * WIDE, 128), WIDE)
        hidden[:, columns] = jnp.transpose(units).astype(BF16)

    for second in kinds:
        third_axis(0, second)
    third_axis(1, 0)
    for second in kinds:
        third_axis(1, second)
    swap_x.wait()
    third_axis(2, 0, (0, 2))
    swiglu(me["y"])
    for order, second in enumerate(kinds):
        third_axis(2, second, (0, 2))
        if order == 2:
            for step in (0,) + kinds:
                third_axis(2, step, (1,))
        swiglu((me["y"] + second + SIDE) % SIDE)

    def swap_out(index):
        columns = pl.ds(pl.multiple_of(index * 256, 256), 256)
        return pltpu.make_async_remote_copy(
            src_ref=other_send.at[:, columns],
            dst_ref=other_recv.at[:, columns],
            send_sem=out_sem.at[0, index],
            recv_sem=out_sem.at[1, index],
            device_id=device_at(sibling),
            device_id_type=MESH,
        )

    def project_down(index, carry):
        columns = pl.ds(pl.multiple_of(index * 256, 256), 256)
        pair = jnp.concatenate([wd[2 * index], wd[2 * index + 1]], axis=1)
        acc[:, columns] = dot(hidden[...], pair)
        other_send[:, columns] = acc[other_rows, columns].astype(BF16)
        swap_out(index).start()
        return carry

    lax.fori_loop(0, WIDTH // 256, project_down, 0)

    def finish(index, carry):
        columns = pl.ds(pl.multiple_of(index * 256, 256), 256)
        swap_out(index).wait()
        mlp = (acc[own_rows, columns] + other_recv[:, columns].astype(F32)).astype(BF16)
        result = resident[:, columns].astype(F32) + mlp.astype(F32)
        out[:, columns] = jnp.where(valid > 0.0, result, 0.0).astype(BF16)
        return carry

    lax.fori_loop(0, WIDTH // 256, finish, 0)

    exchanged(decay_out, decay_in, 0).wait_send()
    exchanged(state_out, state_in, 1).wait_send()
    exchanged(before, incoming, 2).wait_send()
    for part in range(3):
        pairs[part].wait_send()
        sent = w_attn.at[pl.ds(0, 66 * 16), pl.ds(0, 21 * 128)]
        pltpu.make_async_remote_copy(
            src_ref=sent,
            dst_ref=sent,
            send_sem=send_sem.at[part],
            recv_sem=recv_sem.at[part, 0],
            device_id=device_at(sibling),
            device_id_type=MESH,
        ).wait_send()


def layer(lengths, vmem_args, hbm_args):
    vmem = pl.BlockSpec(memory_space=pltpu.VMEM)
    hbm = pl.BlockSpec(memory_space=pltpu.HBM)
    dma = pltpu.SemaphoreType.DMA
    return pl.pallas_call(
        layer_kernel,
        out_shape=jax.ShapeDtypeStruct((ROWS, WIDTH), BF16),
        in_specs=[pl.BlockSpec(memory_space=pltpu.SMEM)]
        + [vmem] * len(vmem_args)
        + [hbm] * len(hbm_args),
        out_specs=vmem,
        scratch_shapes=[
            pltpu.VMEM((SIDE * SIDE, SIDE * HALF, 128), BF16),
            pltpu.VMEM((SIDE * SIDE, SIDE * HALF, 128), BF16),
            pltpu.VMEM((SIDE * SIDE, SIDE * WIDE, 128), BF16),
            pltpu.VMEM((3, QUARTER, 128), BF16),
            pltpu.VMEM((3, HALF, 128), BF16),
            pltpu.VMEM((WIDTH, 2 * KEYS + 2 * VALUES), BF16),
            pltpu.VMEM((VALUES, WIDTH), BF16),
            pltpu.VMEM((ROWS, WIDTH), BF16),
            pltpu.VMEM((HALO + ROWS, 2 * KEYS + VALUES), BF16),
            pltpu.VMEM((ROWS, VALUES), F32),
            pltpu.VMEM((ROWS // SUB, SUB, KEYS), F32),
            pltpu.VMEM((ROWS // SUB, SUB, KEYS), F32),
            pltpu.VMEM((ROWS, VALUES), BF16),
            pltpu.VMEM((ROWS // SUB, SUB, KEYS), F32),
            pltpu.VMEM((KEYS, VW), BF16),
            pltpu.VMEM((KEYS, 128), F32),
            pltpu.VMEM((KEYS, VW), BF16),
            pltpu.VMEM((KEYS, 128), F32),
            pltpu.VMEM((KEYS, VW), BF16),
            pltpu.VMEM((KEYS, VW), BF16),
            pltpu.VMEM((HEADS, ROWS, ROWS), F32),
            pltpu.VMEM((ROWS, VALUES), BF16),
            pltpu.VMEM((ROWS, WIDTH), BF16),
            pltpu.VMEM((WIDTH, 2 * ROWS), BF16),
            pltpu.VMEM((2 * ROWS, SIDE * WIDE), BF16),
            pltpu.VMEM((2 * ROWS, WIDTH), F32),
            pltpu.VMEM((ROWS, WIDTH), BF16),
            pltpu.VMEM((ROWS, WIDTH), BF16),
            dma((5,)),
            dma((3,)),
            dma((3,)),
            dma((3,)),
            dma((3, BLOCKS)),
            dma((2,)),
            dma((6,)),
            dma((2,)),
            dma((2, WIDTH // 256)),
        ],
        compiler_params=pltpu.CompilerParams(
            collective_id=0, has_side_effects=True, vmem_limit_bytes=VMEM_LIMIT
        ),
        name="layer",
    )(lengths, *vmem_args, *hbm_args)


def shards(
    tokens,
    lengths,
    attn_gain,
    w_query,
    w_key,
    w_value,
    w_outgate,
    gate_down,
    gate_up,
    gate_bias,
    conv_weight,
    head_gain,
    w_out,
    forward_norm_scale,
    w_gate,
    w_up,
    down_weight,
):
    rows = [attn_gain, forward_norm_scale, gate_bias, head_gain]
    vectors = jnp.stack([jnp.pad(row.astype(F32), (0, WIDTH - row.shape[0])) for row in rows])
    output = layer(
        lengths,
        (
            tokens[0],
            vectors,
            gate_down.T,
            gate_up,
            conv_weight,
            w_gate,
            w_up,
            down_weight,
        ),
        (w_query, w_key, w_value, w_outgate, w_out),
    )
    return output[None]


def solution(mesh):
    return jax.shard_map(
        shards,
        mesh=mesh,
        in_specs=(P("req", "seq", None),) + (P(),) * 13 + (P("seq", "req"),) * 3,
        out_specs=P("req", "seq", None),
        check_vma=False,
    )
```

```python
import jax
import jax.numpy as jnp
from jax import lax
from jax.experimental import pallas as pl
from jax.experimental.pallas import tpu as pltpu
from jax.sharding import PartitionSpec as P

HEADS = 2
EPSILON = 1e-05
NORMALIZER = 16.0
HIGHEST = lax.Precision.HIGHEST
MESH = pl.DeviceIdType.MESH
F32 = jnp.float32
BF16 = jnp.bfloat16

SIDE = 4
BLOCKS = SIDE**3
DEVICES = 2 * SIDE * SIDE
HALF = 352
WIDE = 384
QUARTER = 2 * HALF
ROWS = 128
SUB = 16
HALO = 16
WIDTH = 2048
KEYS = 512
VALUES = 1024
KW = KEYS // HEADS
VW = VALUES // HEADS
CHIPS = SIDE * SIDE
PIECE = KW // CHIPS
REQUESTS = 4
VMEM_LIMIT = 56 * 2**20
ORDERS = (("x", "y", "z"), ("z", "x", "y"), ("y", "z", "x"))


def place():
    seq = lax.axis_index("seq")
    return {
        "x": seq // (2 * SIDE),
        "z": (seq // 2) % SIDE,
        "y": lax.axis_index("req"),
        "c": seq % 2,
    }


def device_at(at):
    return (at["y"], (at["x"] * SIDE + at["z"]) * 2 + at["c"])


def moved(at, axis, by):
    new = dict(at)
    new[axis] = (at[axis] + by + SIDE) % SIDE
    return new


def dot(a, b):
    return jnp.dot(a, b, preferred_element_type=F32)


def dot_nt(a, b):
    return lax.dot_general(a, b, (((1,), (1,)), ((), ())), preferred_element_type=F32)


def split(a):
    high = a.astype(BF16)
    return high, (a - high.astype(F32)).astype(BF16)


def silu(a):
    return a * jax.nn.sigmoid(a)


def layer_kernel(
    lengths,
    attn_gain,
    forward_scale,
    gate_bias,
    head_gain,
    gate_down,
    gate_up,
    conv_weight,
    tokens_hbm,
    gate_shard,
    up_shard,
    down_shard,
    w_query,
    w_key,
    w_value,
    w_outgate,
    w_out_hbm,
    out,
    tokens,
    raw,
    wg,
    wu,
    wd,
    turned,
    pair_in,
    w_attn,
    w_out,
    normed,
    proj,
    outgate,
    query,
    keys,
    values,
    total,
    state_own,
    decay_own,
    state_other,
    decay_other,
    state_out,
    decay_out,
    state_in,
    decay_in,
    before,
    chip_incoming,
    incoming,
    scores,
    gated,
    resident,
    x_rows,
    hidden,
    acc,
    other_send,
    other_recv,
    load_sem,
    pair_send,
    pair_recv,
    send_sem,
    recv_sem,
    halo_sem,
    state_sem,
    swap_sem,
    out_sem,
    core_sem,
):
    me = place()
    core = me["c"]
    seq = lax.axis_index("seq")
    req = lax.axis_index("req")
    sibling = dict(me, c=1 - core)
    onward = 1 - 2 * core

    shard_loads = []
    for part, shard in enumerate((gate_shard, up_shard, down_shard)):
        load = pltpu.make_async_copy(shard, raw.at[part], load_sem.at[6 + part])
        load.start()
        shard_loads.append(load)
    load_tokens = pltpu.make_async_copy(tokens_hbm, tokens, load_sem.at[5])
    load_tokens.start()
    loads = []
    for index, (source, first, count) in enumerate(
        (
            (w_query, 0, KEYS),
            (w_key, KEYS, KEYS),
            (w_value, 2 * KEYS, VALUES),
            (w_outgate, 2 * KEYS + VALUES, VALUES),
        )
    ):
        load = pltpu.make_async_copy(
            source, w_attn.at[:, pl.ds(first, count)], load_sem.at[index]
        )
        load.start()
        loads.append(load)
    load_out = pltpu.make_async_copy(w_out_hbm, w_out, load_sem.at[4])
    load_out.start()

    barrier = pltpu.get_barrier_semaphore()

    def greet(step, carry):
        pl.semaphore_signal(
            barrier, inc=1, device_id=(req, (seq + 2 * step) % DEVICES), device_id_type=MESH
        )
        return carry

    lax.fori_loop(1, CHIPS, greet, 0)
    for by in (1, DEVICES - 1):
        pl.semaphore_signal(
            barrier, inc=1, device_id=(req, (seq + by) % DEVICES), device_id_type=MESH
        )
    for by in (1, -1):
        pl.semaphore_signal(
            barrier, inc=1, device_id=device_at(moved(me, "y", by)), device_id_type=MESH
        )
    for part in range(3):
        shard_loads[part].wait()
        columns = jnp.transpose(raw[part].astype(F32))
        zeros = jnp.zeros_like(columns)
        turned[part] = jnp.where(
            core == 0,
            jnp.concatenate([columns, zeros], axis=1),
            jnp.concatenate([zeros, columns], axis=1),
        ).astype(BF16)
    pl.semaphore_wait(barrier, CHIPS + 3)

    fulls = (wg, wu, wd)
    strides = (HALF, HALF, WIDE)

    def slot(part, at):
        first = pl.multiple_of(at["y"] * strides[part], 32)
        return fulls[part].at[at["x"] * SIDE + at["z"], pl.ds(first, HALF), :]

    pairs = []
    for part in range(3):
        pair = pltpu.make_async_remote_copy(
            src_ref=turned.at[part, pl.ds(pl.multiple_of((1 - core) * HALF, 32), HALF), :],
            dst_ref=pair_in.at[part],
            send_sem=pair_send.at[part],
            recv_sem=pair_recv.at[part],
            device_id=device_at(sibling),
            device_id_type=MESH,
        )
        pair.start()
        pairs.append(pair)

    def block_of(at):
        return (at["y"] * SIDE + at["x"]) * SIDE + at["z"]

    def copy_of(part, at, axis, by):
        return pltpu.make_async_remote_copy(
            src_ref=slot(part, at),
            dst_ref=slot(part, at),
            send_sem=send_sem.at[part],
            recv_sem=recv_sem.at[part, block_of(at)],
            device_id=device_at(moved(me, axis, by)),
            device_id_type=MESH,
        )

    def send(part, at, axis, by):
        copy_of(part, at, axis, by).start()

    def both(part, at, axis):
        send(part, at, axis, 1)
        send(part, at, axis, -1)

    def arrive(part, at):
        copy_of(part, at, "x", 1).wait_recv()

    kinds = (-onward, onward, 2)

    def at_of(part, *steps):
        at = dict(me)
        for axis, by in zip(ORDERS[part], steps):
            at[axis] = (me[axis] + by + SIDE) % SIDE
        return at

    def first_axis(kind):
        for part in range(3):
            at = at_of(part, kinds[kind])
            arrive(part, at)
            if kind == 0:
                send(part, at, ORDERS[part][0], onward)
            both(part, at, ORDERS[part][1])
            both(part, at, ORDERS[part][2])

    def offset(step):
        side = jnp.where(step == 1, -onward, onward)
        return jnp.where(step == 0, 0, jnp.where(step == 3, 2, side))

    def second_axis(kind):
        def step_(step, carry):
            for part in range(3):
                at = at_of(part, offset(step), kinds[kind])
                arrive(part, at)
                if kind == 0:
                    send(part, at, ORDERS[part][1], onward)
                both(part, at, ORDERS[part][2])
            return carry

        lax.fori_loop(0, SIDE, step_, 0)

    def third_axis(kind, second, parts=(0, 1, 2)):
        def step_(step, carry):
            for part in parts:
                at = at_of(part, offset(step), second, kinds[kind])
                arrive(part, at)
                if kind == 0:
                    send(part, at, ORDERS[part][2], onward)
            return carry

        lax.fori_loop(0, SIDE, step_, 0)

    for part in range(3):
        pairs[part].wait_recv()
        own = turned[part, pl.ds(pl.multiple_of(core * HALF, 32), HALF), :]
        block = slot(part, me)
        block[...] = own + pair_in[part]
        both(part, me, ORDERS[part][0])
    for part in range(3):
        both(part, me, ORDERS[part][1])
    for part in range(3):
        both(part, me, ORDERS[part][2])

    load_tokens.wait()
    inputs = tokens[...].astype(F32)
    mean_square = jnp.mean(inputs * inputs, axis=-1, keepdims=True)
    normed[...] = (
        inputs * lax.rsqrt(mean_square + EPSILON) * attn_gain[...].astype(F32).reshape(1, WIDTH)
    ).astype(BF16)

    for quarter in range(SIDE):
        wd[:, quarter * WIDE + HALF : (quarter + 1) * WIDE, :] = jnp.zeros(
            (SIDE * SIDE, WIDE - HALF, 128), BF16
        )

    def project(index, carry):
        columns = pl.ds(pl.multiple_of(index * 256, 256), 256)
        proj[pl.ds(HALO, ROWS), columns] = dot(normed[...], w_attn[:, columns]).astype(BF16)
        return carry

    loads[0].wait()
    loads[1].wait()
    lax.fori_loop(0, 4, project, 0)
    loads[2].wait()
    lax.fori_loop(4, 8, project, 0)
    halo = pltpu.make_async_remote_copy(
        src_ref=proj.at[pl.ds(ROWS, HALO), :],
        dst_ref=proj.at[pl.ds(0, HALO), :],
        send_sem=halo_sem.at[0],
        recv_sem=halo_sem.at[1],
        device_id=(req, (seq + 1) % DEVICES),
        device_id_type=MESH,
    )
    halo.start()

    for kind in range(3):
        first_axis(kind)

    def project_gate(index, carry):
        source = pl.ds(pl.multiple_of(index * 256 + 2 * KEYS + VALUES, 256), 256)
        target = pl.ds(pl.multiple_of(index * 256, 256), 256)
        outgate[:, target] = dot(normed[...], w_attn[:, source])
        return carry

    loads[3].wait()
    lax.fori_loop(0, 4, project_gate, 0)
    latent = dot_nt(normed[...], gate_down[...])
    logits = (
        jnp.dot(latent, gate_up[...].astype(F32), precision=HIGHEST, preferred_element_type=F32)
        + gate_bias[...].reshape(1, KEYS)
    )
    log_decay = (jnp.minimum(logits, 0.0) - jnp.log1p(jnp.exp(-jnp.abs(logits)))) / NORMALIZER
    row = lax.broadcasted_iota(jnp.int32, (ROWS, ROWS), 0)
    lane = lax.broadcasted_iota(jnp.int32, (ROWS, ROWS), 1)
    lower = (row >= lane).astype(F32)
    cumulative = jnp.dot(lower, log_decay, precision=HIGHEST, preferred_element_type=F32)
    total[...] = cumulative.reshape(ROWS // SUB, SUB, KEYS)
    bounds = [lengths[req, 0]]
    for slot_index in range(1, REQUESTS):
        bounds.append(bounds[-1] + lengths[req, slot_index])

    def segment_of(position):
        count = jnp.zeros_like(position)
        for bound in bounds:
            count = count + (position >= bound).astype(jnp.int32)
        return jnp.where(position < 0, -1, count)

    def column_mask(same):
        return same.astype(F32)[:, :1]

    position = seq * ROWS + row
    segment = segment_of(position)
    allowed = ((segment == segment_of(seq * ROWS + lane)) & (row >= lane)).astype(F32)
    taps_same = [None] + [column_mask(segment_of(position - tap) == segment) for tap in (1, 2, 3)]
    last_segment = segment_of(jnp.zeros_like(row) + (seq * ROWS + ROWS - 1))
    keep = column_mask(segment == last_segment)
    clean = column_mask(segment == segment_of(jnp.zeros_like(row) + (seq * ROWS - 1)))
    valid = column_mask(segment < REQUESTS)
    clean_block = clean[ROWS - 1 : ROWS]
    tail_rows = jnp.dot(
        jnp.transpose(log_decay), jnp.ones((ROWS, 128), F32), precision=HIGHEST,
        preferred_element_type=F32,
    )
    decay_own[...] = jnp.exp(tail_rows) * clean_block

    halo.wait()
    for chunk in range(4):
        columns = slice(chunk * 512, (chunk + 1) * 512)
        rows = proj[:, columns].astype(F32)
        taps = conv_weight[:, columns].astype(F32)
        mixed = rows[HALO:] * taps[0:1]
        for tap in range(1, 4):
            shifted = pltpu.roll(rows, tap, 0)[HALO:]
            mixed = mixed + taps[tap : tap + 1] * jnp.where(taps_same[tap] > 0.0, shifted, 0.0)
        mixed = silu(mixed).astype(BF16)
        if chunk == 0:
            query[...] = mixed.astype(F32).reshape(ROWS // SUB, SUB, KEYS)
        elif chunk == 1:
            keys[...] = mixed.astype(F32).reshape(ROWS // SUB, SUB, KEYS)
        else:
            values[:, (chunk - 2) * 512 : (chunk - 1) * 512] = mixed

    tail = cumulative[ROWS - 1 : ROWS]
    keys_left = (
        keys[...].reshape(ROWS, KEYS) * jnp.exp(tail - cumulative) * keep
    )
    for head in range(HEADS):
        high, low = split(jnp.transpose(keys_left[:, head * KW : (head + 1) * KW]))
        head_values = values[:, head * VW : (head + 1) * VW]
        state_own[head * KW : (head + 1) * KW, :] = (
            dot(high, head_values) + dot(low, head_values)
        ).astype(BF16)

    def to_sibling(source, target, which):
        return pltpu.make_async_remote_copy(
            src_ref=source,
            dst_ref=target,
            send_sem=core_sem.at[0, which],
            recv_sem=core_sem.at[1, which],
            device_id=device_at(sibling),
            device_id_type=MESH,
        )

    swap_state = to_sibling(state_own, state_other, 0)
    swap_state.start()
    swap_decay = to_sibling(decay_own, decay_other, 1)
    swap_decay.start()

    def piece_of(ref, index):
        return ref.at[pl.ds(pl.multiple_of(index * PIECE, PIECE), PIECE), :]

    def exchange(source, target, which):
        def step_(step, carry):
            to = (seq + 2 * step) % DEVICES
            pltpu.make_async_remote_copy(
                src_ref=piece_of(source, to // 2),
                dst_ref=piece_of(target, seq // 2),
                send_sem=state_sem.at[2 * which],
                recv_sem=state_sem.at[2 * which + 1],
                device_id=(req, to),
                device_id_type=MESH,
            ).start()
            return carry

        lax.fori_loop(1, CHIPS, step_, 0)

    def exchanged(source, target, which):
        count = (CHIPS - 1) * PIECE
        return pltpu.make_async_remote_copy(
            src_ref=source.at[pl.ds(0, count), :],
            dst_ref=target.at[pl.ds(0, count), :],
            send_sem=state_sem.at[2 * which],
            recv_sem=state_sem.at[2 * which + 1],
            device_id=device_at(sibling),
            device_id_type=MESH,
        )

    def wide_decay(decay):
        return jnp.concatenate([decay] * (VW // 128), axis=1)

    head_rows = pl.ds(pl.multiple_of(core * KW, KW), KW)
    swap_state.wait_recv()
    swap_decay.wait_recv()
    own_state = state_own[head_rows, :].astype(F32)
    own_decay = decay_own[head_rows, :]
    other_state = state_other[head_rows, :].astype(F32)
    other_decay = decay_other[head_rows, :]
    first = core == 0
    earlier = jnp.where(first, own_state, other_state)
    later = jnp.where(first, other_state, own_state)
    later_decay = jnp.where(first, other_decay, own_decay)
    state_out[...] = (earlier * wide_decay(later_decay) + later).astype(BF16)
    decay_out[...] = own_decay * other_decay

    exchange(decay_out, decay_in, 0)
    exchange(state_out, state_in, 1)
    mine = pl.ds(pl.multiple_of((seq // 2) * PIECE, PIECE), PIECE)
    decay_in[mine, :] = decay_out[mine, :]
    state_in[mine, :] = state_out[mine, :]

    second_axis(0)

    scores[...] = jnp.zeros_like(scores)
    sub_row = row // SUB

    def diagonal(step, carry):
        key_row = keys[:, pl.ds(step, 1), :]
        total_row = total[:, pl.ds(step, 1), :]
        product = query[...] * key_row * jnp.exp(jnp.minimum(total[...] - total_row, 0.0))
        here = lane == sub_row * SUB + step
        for head in range(HEADS):
            summed = jnp.sum(product[:, :, head * KW : (head + 1) * KW], axis=-1, keepdims=True)
            scores[head] += jnp.where(here, summed.reshape(ROWS, 1), 0.0)
        return carry

    lax.fori_loop(0, SUB, diagonal, 0)
    flat_keys = keys[...].reshape(ROWS, KEYS)
    for sub in range(1, ROWS // SUB):
        base = total[sub - 1, SUB - 1 : SUB, :]
        query_high, query_low = split(query[sub] * jnp.exp(total[sub] - base))
        key_high, key_low = split(flat_keys * jnp.exp(jnp.minimum(base - cumulative, 0.0)))
        for head in range(HEADS):
            part = slice(head * KW, (head + 1) * KW)
            block = (
                dot_nt(query_high[:, part], key_high[:, part])
                + dot_nt(query_high[:, part], key_low[:, part])
                + dot_nt(query_low[:, part], key_high[:, part])
            )
            rows = slice(sub * SUB, (sub + 1) * SUB)
            scores[head, rows, :] += jnp.where(lane[:SUB] < sub * SUB, block, 0.0)

    exchanged(decay_out, decay_in, 0).wait_recv()
    exchanged(state_out, state_in, 1).wait_recv()

    def prefix(step, running):
        rows = pl.ds(pl.multiple_of(step * PIECE, PIECE), PIECE)
        before[rows, :] = running.astype(BF16)
        return running * wide_decay(decay_in[rows, :]) + state_in[rows, :].astype(F32)

    lax.fori_loop(0, CHIPS, prefix, jnp.zeros((PIECE, VW), F32))
    exchange(before, chip_incoming, 2)
    chip_incoming[mine, :] = before[mine, :]

    second_axis(1)
    second_axis(2)
    third_axis(0, 0)

    exchanged(before, chip_incoming, 2).wait_recv()
    incoming[head_rows, :] = chip_incoming[...]
    swap_incoming = pltpu.make_async_remote_copy(
        src_ref=chip_incoming,
        dst_ref=incoming.at[head_rows, :],
        send_sem=core_sem.at[0, 2],
        recv_sem=core_sem.at[1, 2],
        device_id=device_at(sibling),
        device_id_type=MESH,
    )
    swap_incoming.start()
    swap_incoming.wait()
    query_decayed = (
        query[...].reshape(ROWS, KEYS) * jnp.exp(cumulative) * clean
    )
    for head in range(HEADS):
        key_part = slice(head * KW, (head + 1) * KW)
        value_part = slice(head * VW, (head + 1) * VW)
        high, low = split(query_decayed[:, key_part])
        weights = (scores[head] * allowed).astype(BF16)
        before_state = incoming[key_part, :]
        after_first = (
            before_state.astype(F32) * wide_decay(decay_other[key_part, :])
            + state_other[key_part, :].astype(F32)
        ).astype(BF16)
        before_state = jnp.where(first, before_state, after_first)
        attended = (
            dot(weights, values[:, value_part]) + dot(high, before_state) + dot(low, before_state)
        )
        mean_square = jnp.mean(attended * attended, axis=-1, keepdims=True)
        scaled = attended * lax.rsqrt(mean_square + EPSILON) * head_gain[...].astype(F32).reshape(1, VW)
        gated[:, value_part] = (scaled * silu(outgate[:, value_part])).astype(BF16)

    load_out.wait()

    def project_out(index, carry):
        columns = pl.ds(pl.multiple_of(index * 256, 256), 256)
        resident[:, columns] = (
            dot(gated[...], w_out[:, columns]) + tokens[:, columns].astype(F32)
        ).astype(BF16)
        return carry

    lax.fori_loop(0, WIDTH // 256, project_out, 0)
    wide = resident[...].astype(F32)
    mean_square = jnp.mean(wide * wide, axis=-1, keepdims=True)
    own_rows = pl.ds(pl.multiple_of(core * ROWS, ROWS), ROWS)
    other_rows = pl.ds(pl.multiple_of((1 - core) * ROWS, ROWS), ROWS)
    x_rows[:, own_rows] = jnp.transpose(
        wide * lax.rsqrt(mean_square + EPSILON) * forward_scale[...].astype(F32).reshape(1, WIDTH)
    ).astype(BF16)
    swap_x = pltpu.make_async_remote_copy(
        src_ref=x_rows.at[:, own_rows],
        dst_ref=x_rows.at[:, own_rows],
        send_sem=swap_sem.at[0],
        recv_sem=swap_sem.at[1],
        device_id=device_at(sibling),
        device_id_type=MESH,
    )
    swap_x.start()

    def swiglu(quarter):
        rows = pl.ds(pl.multiple_of(quarter * HALF, 32), HALF)

        def product(full):
            summed = None
            for index in range(WIDTH // 256):
                pair = jnp.concatenate([full[2 * index, rows, :], full[2 * index + 1, rows, :]], axis=1)
                term = dot(pair, x_rows[index * 256 : (index + 1) * 256, :])
                summed = term if summed is None else summed + term
            return summed

        units = silu(product(wg)) * product(wu)
        units = jnp.concatenate([units, jnp.zeros((WIDE - HALF, 2 * ROWS), F32)], axis=0)
        columns = pl.ds(pl.multiple_of(quarter * WIDE, 128), WIDE)
        hidden[:, columns] = jnp.transpose(units).astype(BF16)

    for second in kinds:
        third_axis(0, second)
    third_axis(1, 0)
    for second in kinds:
        third_axis(1, second)
    swap_x.wait()
    third_axis(2, 0, (0, 2))
    swiglu(me["y"])
    for order, second in enumerate(kinds):
        third_axis(2, second, (0, 2))
        if order == 2:
            for step in (0,) + kinds:
                third_axis(2, step, (1,))
        swiglu((me["y"] + second + SIDE) % SIDE)

    def swap_out(index):
        columns = pl.ds(pl.multiple_of(index * 256, 256), 256)
        return pltpu.make_async_remote_copy(
            src_ref=other_send.at[:, columns],
            dst_ref=other_recv.at[:, columns],
            send_sem=out_sem.at[0, index],
            recv_sem=out_sem.at[1, index],
            device_id=device_at(sibling),
            device_id_type=MESH,
        )

    def project_down(index, carry):
        columns = pl.ds(pl.multiple_of(index * 256, 256), 256)
        pair = jnp.concatenate([wd[2 * index], wd[2 * index + 1]], axis=1)
        acc[:, columns] = dot(hidden[...], pair)
        other_send[:, columns] = acc[other_rows, columns].astype(BF16)
        swap_out(index).start()
        return carry

    lax.fori_loop(0, WIDTH // 256, project_down, 0)

    def finish(index, carry):
        columns = pl.ds(pl.multiple_of(index * 256, 256), 256)
        swap_out(index).wait()
        mlp = (acc[own_rows, columns] + other_recv[:, columns].astype(F32)).astype(BF16)
        result = resident[:, columns].astype(F32) + mlp.astype(F32)
        out[:, columns] = jnp.where(valid > 0.0, result, 0.0).astype(BF16)
        return carry

    lax.fori_loop(0, WIDTH // 256, finish, 0)

    exchanged(decay_out, decay_in, 0).wait_send()
    exchanged(state_out, state_in, 1).wait_send()
    exchanged(before, chip_incoming, 2).wait_send()
    swap_state.wait_send()
    swap_decay.wait_send()
    for part in range(3):
        pairs[part].wait_send()
        sent = w_attn.at[pl.ds(0, 66 * 16), pl.ds(0, 21 * 128)]
        pltpu.make_async_remote_copy(
            src_ref=sent,
            dst_ref=sent,
            send_sem=send_sem.at[part],
            recv_sem=recv_sem.at[part, 0],
            device_id=device_at(sibling),
            device_id_type=MESH,
        ).wait_send()


def layer(lengths, vmem_args, hbm_args):
    vmem = pl.BlockSpec(memory_space=pltpu.VMEM)
    hbm = pl.BlockSpec(memory_space=pltpu.HBM)
    dma = pltpu.SemaphoreType.DMA
    return pl.pallas_call(
        layer_kernel,
        out_shape=jax.ShapeDtypeStruct((ROWS, WIDTH), BF16),
        in_specs=[pl.BlockSpec(memory_space=pltpu.SMEM)]
        + [vmem] * len(vmem_args)
        + [hbm] * len(hbm_args),
        out_specs=vmem,
        scratch_shapes=[
            pltpu.VMEM((ROWS, WIDTH), BF16),
            pltpu.VMEM((3, 64, QUARTER), BF16),
            pltpu.VMEM((SIDE * SIDE, SIDE * HALF, 128), BF16),
            pltpu.VMEM((SIDE * SIDE, SIDE * HALF, 128), BF16),
            pltpu.VMEM((SIDE * SIDE, SIDE * WIDE, 128), BF16),
            pltpu.VMEM((3, QUARTER, 128), BF16),
            pltpu.VMEM((3, HALF, 128), BF16),
            pltpu.VMEM((WIDTH, 2 * KEYS + 2 * VALUES), BF16),
            pltpu.VMEM((VALUES, WIDTH), BF16),
            pltpu.VMEM((ROWS, WIDTH), BF16),
            pltpu.VMEM((HALO + ROWS, 2 * KEYS + VALUES), BF16),
            pltpu.VMEM((ROWS, VALUES), F32),
            pltpu.VMEM((ROWS // SUB, SUB, KEYS), F32),
            pltpu.VMEM((ROWS // SUB, SUB, KEYS), F32),
            pltpu.VMEM((ROWS, VALUES), BF16),
            pltpu.VMEM((ROWS // SUB, SUB, KEYS), F32),
            pltpu.VMEM((KEYS, VW), BF16),
            pltpu.VMEM((KEYS, 128), F32),
            pltpu.VMEM((KEYS, VW), BF16),
            pltpu.VMEM((KEYS, 128), F32),
            pltpu.VMEM((KW, VW), BF16),
            pltpu.VMEM((KW, 128), F32),
            pltpu.VMEM((KW, VW), BF16),
            pltpu.VMEM((KW, 128), F32),
            pltpu.VMEM((KW, VW), BF16),
            pltpu.VMEM((KW, VW), BF16),
            pltpu.VMEM((KEYS, VW), BF16),
            pltpu.VMEM((HEADS, ROWS, ROWS), F32),
            pltpu.VMEM((ROWS, VALUES), BF16),
            pltpu.VMEM((ROWS, WIDTH), BF16),
            pltpu.VMEM((WIDTH, 2 * ROWS), BF16),
            pltpu.VMEM((2 * ROWS, SIDE * WIDE), BF16),
            pltpu.VMEM((2 * ROWS, WIDTH), F32),
            pltpu.VMEM((ROWS, WIDTH), BF16),
            pltpu.VMEM((ROWS, WIDTH), BF16),
            dma((9,)),
            dma((3,)),
            dma((3,)),
            dma((3,)),
            dma((3, BLOCKS)),
            dma((2,)),
            dma((6,)),
            dma((2,)),
            dma((2, WIDTH // 256)),
            dma((2, 3)),
        ],
        compiler_params=pltpu.CompilerParams(
            collective_id=0, has_side_effects=True, vmem_limit_bytes=VMEM_LIMIT
        ),
        name="layer",
    )(lengths, *vmem_args, *hbm_args)


def shards(
    tokens,
    lengths,
    attn_gain,
    w_query,
    w_key,
    w_value,
    w_outgate,
    gate_down,
    gate_up,
    gate_bias,
    conv_weight,
    head_gain,
    w_out,
    forward_norm_scale,
    w_gate,
    w_up,
    down_weight,
):
    output = layer(
        lengths,
        (attn_gain, forward_norm_scale, gate_bias, head_gain, gate_down.T, gate_up, conv_weight),
        (
            tokens[0],
            w_gate,
            w_up,
            down_weight,
            w_query,
            w_key,
            w_value,
            w_outgate,
            w_out,
        ),
    )
    return output[None]


def solution(mesh):
    return jax.shard_map(
        shards,
        mesh=mesh,
        in_specs=(P("req", "seq", None),) + (P(),) * 13 + (P("seq", "req"),) * 3,
        out_specs=P("req", "seq", None),
        check_vma=False,
    )
```
